512 devices in a mesh: dom: 128 (over z, x, core), face: 4 (over y).
Axes of the slice: x: 4, y: 4, z: 16, core: 2. Of those that a mesh axis runs over, the one named last changes fastest.
Arguments:
- start: float32 [64, 65536], P(None, ('dom', 'face')), may hold values from -6 to 6
- rhs: float32 [64, 65536], P(None, ('dom', 'face')), may hold values from -6 to 6
- diag_block: bfloat16 [64, 64, 65536], P(None, None, ('dom', 'face'))
- precond: bfloat16 [64, 64, 65536], P(None, None, ('dom', 'face'))
- lift: float32 [6, 16, 64], replicated, may hold values from -0.625 to 0.625
- neighbour: int32 [6, 65536], P(None, ('dom', 'face')), may hold values from 0 to 831, as said below
- orient: int32 [6, 65536], P(None, ('dom', 'face')), may hold values from 0 to 7
- owner: int32 [65536], P(('dom', 'face')), may hold values from 0 to 127, as said below
- slot: int32 [65536], P(('dom', 'face')), may hold values from 0 to 63
Outputs:
- solution: float32 [64, 65536], P(None, ('dom', 'face'))
- coarse_op: float32 [729, 32768], P(None, ('dom', 'face'))
- coarse_rhs: float32 [27, 32768], P(None, ('dom', 'face'))
The draws below stay inside these ranges and needn't reach their ends.
Inputs may be any that keep to these rules, and one draw needn't show every extreme that they name: neighbour of face 2 of local element e < 32 is 768 + e; of face 3 of local element 128 - 32 + j it is 800 + j; every other face f points to a face-(f xor 1) trace of a local element, below 768. Local elements 0 .. 31 of a device are owned by its own dom index, all others by another dom index; from the elements of one device at most 2 go to one owner, and some owner receives exactly 2 from each device.
All inputs are finite; a program needn't handle non-finite values.
Results may differ from the reference program's by a relative error of at most 0.0029.
Values may be sent and summed in bfloat16 or wider, within the bound.
A program may use at most 64 MiB of HBM per device.

```python
import jax
import jax.numpy as jnp
import numpy as np
from jax import lax

NODES = 64
FACE_NODES = 16
SWEEPS = 2
E_DEV = 128
STAYING = 32
BOUNDARY = 32
AGG_DEV = 64
OWNER_RANKS = 128
SLABS = 4
CAPACITY = 2
ELEMENTS = 65536
AGGREGATES = 32768


def block_draw(key, diag_lo, diag_hi, spread):
    first, second = jax.random.split(key)
    offdiag = spread * jax.random.normal(first, (64, 64, ELEMENTS), jnp.float32)
    diagonal = jax.random.uniform(second, (64, ELEMENTS), jnp.float32, diag_lo, diag_hi)
    identity = jnp.eye(64, dtype=jnp.float32)[:, :, None]
    return offdiag * (1.0 - identity) + identity * diagonal[:, None, :]


def draw_diag_block(key, part):
    return block_draw(key, 3.0, 5.0, 0.15).astype(jnp.bfloat16)


def draw_precond(key, part):
    return block_draw(key, 0.15, 0.3, 0.02).astype(jnp.bfloat16)


def draw_neighbour(key, part):
    element = jnp.arange(ELEMENTS, dtype=jnp.int32)
    local_pos = element % E_DEV
    rows_out = []
    for direction in range(6):
        random_elem = jax.random.randint(jax.random.fold_in(key, direction), (ELEMENTS,), 0, E_DEV)
        chosen = (direction ^ 1) * E_DEV + random_elem
        if direction == 2:
            chosen = jnp.where(local_pos < BOUNDARY, 6 * E_DEV + local_pos, chosen)
        if direction == 3:
            chosen = jnp.where(local_pos >= E_DEV - BOUNDARY, 6 * E_DEV + BOUNDARY + local_pos - (E_DEV - BOUNDARY), chosen)
        rows_out.append(chosen)
    return jnp.stack(rows_out).astype(jnp.int32)


def routing(key):
    root_key = jax.random.fold_in(key, 77)
    jitter_key, extra_key, pinned_key, placement_key = jax.random.split(root_key, 4)
    devices = OWNER_RANKS * SLABS
    dom_of = jnp.arange(devices, dtype=jnp.int32) // SLABS
    cells = (OWNER_RANKS - 1) * CAPACITY
    movers = E_DEV - STAYING
    jitter_values = jax.random.randint(jitter_key, (devices, cells), 0, 65536)
    favoured_owners = jax.random.randint(extra_key, (OWNER_RANKS,), 0, 4)
    pinned_owner = jax.random.randint(pinned_key, (devices,), 1, OWNER_RANKS)
    cell_numbers = jnp.arange(cells, dtype=jnp.int32)
    shift_amount = cell_numbers // CAPACITY + 1
    destination = (dom_of[:, None] + shift_amount[None, :]) % OWNER_RANKS
    extra_score = favoured_owners[destination] + 8 * (shift_amount[None, :] == pinned_owner[:, None]).astype(jnp.int32)
    ranking_score = (extra_score * 65536 + jitter_values) * 1024 + cell_numbers[None, :]
    unused, picked = lax.top_k(ranking_score, movers)
    moving_dest = (dom_of[:, None] + picked // CAPACITY + 1) % OWNER_RANKS
    staying_dest = jnp.broadcast_to(dom_of[:, None], (devices, STAYING))
    owners_all = jnp.concatenate([staying_dest, moving_dest], 1).reshape(-1).astype(jnp.int32)
    slots_all = jax.random.randint(placement_key, (devices, E_DEV), 0, AGG_DEV)
    position = jnp.arange(E_DEV, dtype=jnp.int32)[None, :]
    slots_all = jnp.where(position == 0, 0, slots_all)
    slots_all = jnp.where(position == E_DEV - 1, AGG_DEV - 1, slots_all)
    return (owners_all, slots_all.reshape(-1).astype(jnp.int32))


def draw_owner(key, part):
    return routing(key)[0]


def draw_slot(key, part):
    return routing(key)[1]


def plant(result, own_key, smallest, top_value):
    shape = result.shape
    place = [jax.random.randint(jax.random.fold_in(own_key, axis), (), 0, shape[axis]) for axis in range(len(shape))]
    result = result.at[tuple(place)].set(smallest)
    longest = shape.index(max(shape))
    place[longest] = (place[longest] + 1) % shape[longest]
    return result.at[tuple(place)].set(top_value)


def level_of(own_key, shape, shards, smallest, high):
    def one(dim, shards_of):
        steps = jax.random.uniform(jax.random.fold_in(jax.random.fold_in(own_key, 6), dim), (shards_of,), jnp.float32, smallest / len(shards), high / len(shards))
        return jnp.repeat(jnp.exp(steps), shape[dim] // shards_of).reshape((-1,) + (1,) * (len(shape) - dim - 1))

    loudness = one(*shards[0])
    for cut in shards[1:]:
        loudness = loudness * one(*cut)
    return loudness


def noise(stream_key, shape, scale, reach, cuts=(), kind=jnp.bfloat16):
    values = jax.random.normal(stream_key, shape, jnp.float32) * scale
    if len(cuts) > 0:
        values = level_of(stream_key, shape, cuts, -0.22, 0.18) * values
    return jnp.clip(values, min=-reach, max=reach).astype(kind)


def setup_inputs(seed: int = 0) -> dict:
    splits = jax.random.split(jax.random.key(seed), 10)
    start = noise(splits[0], (NODES, ELEMENTS), 1.0, 6.0, ((1, 512),), jnp.float32)
    rhs = noise(splits[1], (NODES, ELEMENTS), 1.0, 6.0, ((1, 512),), jnp.float32)
    diag_block = draw_diag_block(jax.random.fold_in(splits[9], 71), 0)
    precond = draw_precond(jax.random.fold_in(splits[9], 71), 0)
    lift = noise(splits[4], (6, FACE_NODES, NODES), 96 ** -0.5, 0.625, (), jnp.float32)
    neighbour = draw_neighbour(jax.random.fold_in(splits[9], 71), 0)
    orient = plant(jax.random.randint(splits[6], (6, ELEMENTS), 0, 8), jax.random.fold_in(splits[6], 1), 0, 7).astype(jnp.int32)
    owner = draw_owner(jax.random.fold_in(splits[9], 71), 0)
    slot = draw_slot(jax.random.fold_in(splits[9], 71), 0)
    return dict(start=start, rhs=rhs, diag_block=diag_block, precond=precond, lift=lift, neighbour=neighbour, orient=orient, owner=owner, slot=slot)


def turn_table():
    square = np.arange(16).reshape(4, 4)
    tables = []
    for turn in range(8):
        layout = square.T if turn & 4 else square
        if turn & 1:
            layout = layout[::-1, :]
        if turn & 2:
            layout = layout[:, ::-1]
        tables.append(layout.reshape(16))
    return np.stack(tables)

def restrict_table():
    fine_nodes = np.array([-1.0, -1.0 / np.sqrt(5.0), 1.0 / np.sqrt(5.0), 1.0])
    coarse_nodes = np.array([-1.0, 0.0, 1.0])
    basis = np.ones((4, 3))
    for column in range(3):
        for other in range(3):
            if other != column:
                basis[:, column] *= (fine_nodes - coarse_nodes[other]) / (coarse_nodes[column] - coarse_nodes[other])
    prolong = (basis[:, None, None, :, None, None] * basis[None, :, None, None, :, None] * basis[None, None, :, None, None, :]).reshape(64, 27)
    return prolong.T.astype(np.float32)

def face_traces(values):
    cube = values.reshape(4, 4, 4, -1)
    planes = [cube[0], cube[3], cube[:, 0], cube[:, 3], cube[:, :, 0], cube[:, :, 3]]
    return jnp.stack([plane.reshape(16, -1) for plane in planes])

def couple(face_vals, low_in, high_in, neighbour, orient, lift):
    local_count = face_vals.shape[2]
    pool = jnp.concatenate([face_vals.transpose(1, 0, 2).reshape(16, 6 * local_count), low_in, high_in], 1)
    picked = jnp.take(pool, neighbour.reshape(-1), axis=1).reshape(16, 6, local_count)
    tables = turn_table()
    turned = jnp.zeros_like(picked)
    for turn in range(8):
        turned = turned + jnp.where(orient[None, :, :] == turn, picked[tables[turn]], 0.0)
    return jnp.einsum('kfn,fke->ne', lift, turned, precision=lax.Precision.HIGHEST)

def galerkin(blocks, rtab):
    half = jnp.einsum('cn,nms->cms', rtab, blocks, precision=lax.Precision.HIGHEST)
    return jnp.einsum('cms,dm->cds', half, rtab, precision=lax.Precision.HIGHEST)

def reference(start, rhs, diag_block, precond, lift, neighbour, orient, owner, slot):
    devices = OWNER_RANKS * SLABS
    indices = jnp.arange(devices, dtype=jnp.int32)

    def cut(array, index):
        return lax.dynamic_slice_in_dim(array, index * E_DEV, E_DEV, axis=array.ndim - 1)

    def to_global(stacked):
        return stacked.transpose(1, 0, 2).reshape(stacked.shape[1], ELEMENTS)

    def all_residuals(values):

        def rim_of(index):
            face_vals = face_traces(cut(values, index))
            return jnp.concatenate([face_vals[2][:, :BOUNDARY], face_vals[3][:, E_DEV - BOUNDARY:]], 1)
        rims = lax.map(rim_of, indices).reshape(OWNER_RANKS, SLABS, 16, 2 * BOUNDARY)
        blank = jnp.zeros((OWNER_RANKS, 1, 16, BOUNDARY), jnp.float32)
        from_below = jnp.concatenate([blank, rims[:, :-1, :, BOUNDARY:]], 1).reshape(devices, 16, BOUNDARY)
        from_above = jnp.concatenate([rims[:, 1:, :, :BOUNDARY], blank], 1).reshape(devices, 16, BOUNDARY)

        def one_device(inputs):
            index, low_in, high_in = inputs
            local_vals = cut(values, index)
            face_vals = face_traces(local_vals)
            product = jnp.einsum('nme,me->ne', cut(diag_block, index).astype(jnp.float32), local_vals, precision=lax.Precision.HIGHEST)
            coupled = couple(face_vals, low_in, high_in, cut(neighbour, index), cut(orient, index), lift)
            return cut(rhs, index) - (product - coupled)
        return to_global(lax.map(one_device, (indices, from_below, from_above)))
    solution = start
    for sweep_idx in range(SWEEPS):
        resid = all_residuals(solution)

        def smooth(index):
            return jnp.einsum('nme,me->ne', cut(precond, index).astype(jnp.float32), cut(resid, index), precision=lax.Precision.HIGHEST)
        solution = solution + to_global(lax.map(smooth, indices))
    resid = all_residuals(solution)
    resid_low = lax.optimization_barrier(resid.astype(jnp.bfloat16))
    rtab = jnp.asarray(restrict_table(), dtype=jnp.float32)

    def coarse_of(index):
        return galerkin(cut(diag_block, index).astype(jnp.float32), rtab).reshape(729, E_DEV)
    element_coarse = to_global(lax.map(coarse_of, indices))
    element_rhs = jnp.einsum('cn,ne->ce', rtab, resid_low.astype(jnp.float32), precision=lax.Precision.HIGHEST)
    element = jnp.arange(ELEMENTS, dtype=jnp.int32)
    slab_index = element // E_DEV % SLABS
    target = (owner * SLABS + slab_index) * AGG_DEV + slot
    coarse_op = jnp.zeros((729, AGGREGATES), jnp.float32).at[:, target].add(element_coarse)
    coarse_rhs = jnp.zeros((27, AGGREGATES), jnp.float32).at[:, target].add(element_rhs)
    return (solution, coarse_op, coarse_rhs)
```

```python
import functools

import jax
import jax.numpy as jnp
import numpy as np
from jax import lax
from jax.experimental import pallas as pl
from jax.experimental.pallas import tpu as pltpu
from jax.sharding import PartitionSpec as P

SWEEPS = 2
MESH = pl.DeviceIdType.MESH
WIDTHS = (384, 256, 128)
STARTS = (0, 384, 640)
COLS = 768
SLOT_COL = 729
RHS_COL = 736
F32 = jnp.float32
BF16 = jnp.bfloat16


def line_basis():
    fine_nodes = np.array([-1.0, -1.0 / np.sqrt(5.0), 1.0 / np.sqrt(5.0), 1.0])
    coarse_nodes = np.array([-1.0, 0.0, 1.0])
    basis = np.ones((4, 3))
    for column in range(3):
        for other in range(3):
            if other != column:
                basis[:, column] *= (fine_nodes - coarse_nodes[other]) / (
                    coarse_nodes[column] - coarse_nodes[other]
                )
    return basis


def restrict_table():
    basis = line_basis()
    prolong = (
        basis[:, None, None, :, None, None]
        * basis[None, :, None, None, :, None]
        * basis[None, None, :, None, None, :]
    ).reshape(64, 27)
    return prolong.T.astype(np.float32)


def split_restrict():
    table = restrict_table()
    high = table.astype(BF16).astype(np.float32)
    both = np.zeros((64, 64), np.float32)
    both[:27] = high
    both[32:59] = table - high
    return both


def nt(lhs, rhs):
    return lax.dot_general(lhs, rhs, (((1,), (1,)), ((), ())), preferred_element_type=F32)


def mm(lhs, rhs):
    return jnp.dot(lhs, rhs, preferred_element_type=F32)


def halves(value):
    high = value.astype(BF16)
    return high, (value - high.astype(F32)).astype(BF16)


def reduce_line(v0, v1, v2, v3):
    basis = line_basis()
    outs = []
    for column in range(3):
        total = None
        for value, weight in zip((v0, v1, v2, v3), basis[:, column]):
            if weight == 0.0:
                continue
            term = value if weight == 1.0 else value * np.float32(weight)
            total = term if total is None else total + term
        outs.append(total)
    return outs


def kernel(
    nz,
    nxc,
    ny,
    start_ref,
    rhs_ref,
    diag_ref,
    prec_ref,
    lift_ref,
    nb_ref,
    ori_ref,
    own_ref,
    slot_ref,
    rmat_ref,
    sol_ref,
    op_ref,
    crhs_ref,
    line_i,
    coarse,
    val,
    trace,
    lift_t,
    index,
    turn,
    halo_out,
    halo_in,
    product,
    send_z0,
    send_z1,
    send_z2,
    recv_z0,
    recv_z1,
    recv_z2,
    send_x0,
    send_x1,
    send_x2,
    recv_x0,
    recv_x1,
    recv_x2,
    zs_sem,
    zr_sem,
    xs_sem,
    xr_sem,
    hs_sem,
    hr_sem,
):
    send_z = (send_z0, send_z1, send_z2)
    recv_z = (recv_z0, recv_z1, recv_z2)
    send_x = (send_x0, send_x1, send_x2)
    recv_x = (recv_x0, recv_x1, recv_x2)
    dom = lax.axis_index("dom")
    y = lax.axis_index("face")
    z = lax.div(dom, nxc)
    xc = lax.rem(dom, nxc)
    above = lax.rem(y + 1, ny)
    below = lax.rem(y + ny - 1, ny)
    rows = nz * nxc * 2

    barrier = pltpu.get_barrier_semaphore()

    @pl.loop(1, nz)
    def _(step):
        pl.semaphore_signal(
            barrier,
            inc=1,
            device_id=(lax.rem(z + step, nz) * nxc + xc, y),
            device_id_type=MESH,
        )

    @pl.loop(1, nxc)
    def _(step):
        pl.semaphore_signal(
            barrier,
            inc=1,
            device_id=(z * nxc + lax.rem(xc + step, nxc), y),
            device_id_type=MESH,
        )

    for other in (above, below):
        pl.semaphore_signal(barrier, inc=1, device_id=(dom, other), device_id_type=MESH)

    lane = lax.broadcasted_iota(jnp.int32, (1, 128), 1)

    coarse[pl.ds(728, 40), :] = jnp.zeros((40, 128), F32)
    rmat = rmat_ref[...]
    for rest in range(16):
        quad = []
        for i in range(4):
            both = mm(rmat, diag_ref[16 * i + rest])
            quad.append(both[:32] + both[32:])
        for out, value in enumerate(reduce_line(*quad)):
            line_i[out * 16 + rest] = value
    for a in range(3):
        planes = [[], [], []]
        for k in range(4):
            quad = [line_i[a * 16 + 4 * j + k] for j in range(4)]
            for b, value in enumerate(reduce_line(*quad)):
                planes[b].append(value)
        for b in range(3):
            for c, value in enumerate(reduce_line(*planes[b])):
                place = 27 * (9 * a + 3 * b + c)
                coarse[pl.ds(place, 27), :] = value[:27]
    coarse[pl.ds(SLOT_COL, 1), :] = slot_ref[...].astype(F32)

    own = own_ref[...]
    own_cols = jnp.broadcast_to(own, (128, 128))
    own_rows = own_cols.T
    row_id = lax.broadcasted_iota(jnp.int32, (128, 128), 0)
    col_id = lax.broadcasted_iota(jnp.int32, (128, 128), 1)
    same = (own_rows == own_cols) & (row_id >= 32) & (row_id < col_id)
    rank = jnp.sum(jnp.where(same, 1.0, 0.0), axis=0, keepdims=True)
    key = jnp.where(lane >= 32, own * 2 + rank.astype(jnp.int32), -1)
    out_rows = lax.broadcasted_iota(jnp.int32, (rows, 128), 0)
    pick = jnp.where(out_rows == key, 1.0, 0.0).astype(BF16)

    def pack(chunk):
        block = coarse[pl.ds(STARTS[chunk], WIDTHS[chunk]), :].astype(BF16)
        packed = nt(pick, block).astype(BF16)
        send_z[chunk][...] = packed.reshape(nz, nxc * 2, WIDTHS[chunk])

    pack(0)
    pack(1)

    trace[...] = jnp.zeros((128, 128), F32)
    lift_t[...] = jnp.zeros((128, 128), F32)
    for f in range(6):
        lift_t[pl.ds(f, 16, stride=8), :] = lift_ref[f]
    lift_hi, lift_lo = halves(lift_t[...].T[:64])
    index[...] = jnp.zeros((8, 128), jnp.int32)
    turn[...] = jnp.zeros((8, 128), jnp.int32)
    index[pl.ds(0, 6), :] = nb_ref[...] & 127
    turn[pl.ds(0, 6), :] = ori_ref[...]
    idx = index[...]
    flip_row = (turn[...] & 1) != 0
    flip_col = (turn[...] & 2) != 0
    swap = (turn[...] & 4) != 0
    face_id = lax.broadcasted_iota(jnp.int32, (8, 128), 0)
    lane8 = lax.broadcasted_iota(jnp.int32, (8, 128), 1)
    from_low = (face_id == 2) & (lane8 < 32)
    from_high = (face_id == 3) & (lane8 >= 96)

    def halo_copy(turn_no, side):
        other = above if side == 0 else below
        return pltpu.make_async_remote_copy(
            src_ref=halo_out.at[turn_no],
            dst_ref=halo_in.at[turn_no, side],
            send_sem=hs_sem.at[turn_no, side],
            recv_sem=hr_sem.at[turn_no, side],
            device_id=(dom, other),
            device_id_type=MESH,
        )

    def fill_halo(turn_no):
        low = jnp.concatenate([val[pl.ds(16 * i, 4), :] for i in range(4)], 0)
        high = jnp.concatenate([val[pl.ds(16 * i + 12, 4), :] for i in range(4)], 0)
        halo_out[turn_no] = jnp.where(
            lane < 64, pltpu.roll(high, 32, 1), pltpu.roll(low, 96, 1)
        )

    def matvec(matrix_ref, vector):
        for block in range(8):
            part = matrix_ref[pl.ds(8 * block, 8)].astype(F32) * vector[None]
            product[pl.ds(8 * block, 8), :] = jnp.sum(part, axis=1)
        return product[...]

    def coupled(turn_no):
        trace[pl.ds(1, 16, stride=8), :] = val[pl.ds(0, 16), :]
        trace[pl.ds(0, 16, stride=8), :] = val[pl.ds(48, 16), :]
        for i in range(4):
            trace[pl.ds(32 * i + 3, 4, stride=8), :] = val[pl.ds(16 * i, 4), :]
            trace[pl.ds(32 * i + 2, 4, stride=8), :] = val[pl.ds(16 * i + 12, 4), :]
        trace[pl.ds(5, 16, stride=8), :] = val[pl.ds(0, 16, stride=4), :]
        trace[pl.ds(4, 16, stride=8), :] = val[pl.ds(3, 16, stride=4), :]
        for side in range(2):
            halo_copy(turn_no, side).wait_recv()
        low = jnp.where(y > 0, halo_in[turn_no, 0], 0.0)
        high = jnp.where(y < ny - 1, halo_in[turn_no, 1], 0.0)
        cells = []
        for k in range(16):
            cell = jnp.take_along_axis(
                trace[pl.ds(8 * k, 8), :], idx, axis=1, mode="promise_in_bounds"
            )
            cell = jnp.where(from_low, low[k : k + 1], cell)
            cells.append(jnp.where(from_high, high[k : k + 1], cell))
        cells = [jnp.where(swap, cells[4 * (k % 4) + k // 4], cells[k]) for k in range(16)]
        cells = [jnp.where(flip_row, cells[4 * (3 - k // 4) + k % 4], cells[k]) for k in range(16)]
        cells = [jnp.where(flip_col, cells[4 * (k // 4) + 3 - k % 4], cells[k]) for k in range(16)]
        turned_hi, turned_lo = halves(jnp.concatenate(cells, 0))
        return mm(lift_hi, turned_hi) + (mm(lift_hi, turned_lo) + mm(lift_lo, turned_hi))

    val[...] = start_ref[...]
    fill_halo(0)

    pl.semaphore_wait(barrier, nz - 1 + nxc - 1 + 2)

    def send_halo(turn_no):
        for side in range(2):
            halo_copy(turn_no, side).start()

    def z_copy(chunk, other):
        return pltpu.make_async_remote_copy(
            src_ref=send_z[chunk].at[other],
            dst_ref=recv_z[chunk].at[z],
            send_sem=zs_sem.at[chunk, other],
            recv_sem=zr_sem.at[chunk, z],
            device_id=(other * nxc + xc, y),
            device_id_type=MESH,
        )

    def z_arrival(chunk, other):
        return pltpu.make_async_remote_copy(
            src_ref=send_z[chunk].at[other],
            dst_ref=recv_z[chunk].at[other],
            send_sem=zs_sem.at[chunk, other],
            recv_sem=zr_sem.at[chunk, other],
            device_id=(other * nxc + xc, y),
            device_id_type=MESH,
        )

    def x_copy(chunk, other):
        return pltpu.make_async_remote_copy(
            src_ref=send_x[chunk].at[other],
            dst_ref=recv_x[chunk].at[xc],
            send_sem=xs_sem.at[chunk, other],
            recv_sem=xr_sem.at[chunk, xc],
            device_id=(z * nxc + other, y),
            device_id_type=MESH,
        )

    def x_arrival(chunk, other):
        return pltpu.make_async_remote_copy(
            src_ref=send_x[chunk].at[other],
            dst_ref=recv_x[chunk].at[other],
            send_sem=xs_sem.at[chunk, other],
            recv_sem=xr_sem.at[chunk, other],
            device_id=(z * nxc + other, y),
            device_id_type=MESH,
        )

    def start_z(chunk):
        @pl.loop(1, nz)
        def _(step):
            far = lax.div(step, 2)
            shift = jnp.where(lax.rem(step, 2) == 1, nz // 2 - far, nz // 2 + far)
            z_copy(chunk, lax.rem(z + shift, nz)).start()

        recv_z[chunk][z] = send_z[chunk][z]

    def forward(chunk):
        @pl.loop(1, nz)
        def _(step):
            z_arrival(chunk, lax.rem(z + step, nz)).wait_recv()

        to_row = lax.broadcasted_iota(jnp.int32, (rows, rows), 0)
        from_row = lax.broadcasted_iota(jnp.int32, (rows, rows), 1)
        r = lax.rem(to_row, 2)
        src = lax.rem(lax.div(to_row, 2), nz)
        dst = lax.div(to_row, 2 * nz)
        move = jnp.where(from_row == src * (2 * nxc) + dst * 2 + r, 1.0, 0.0).astype(BF16)
        moved = mm(move, recv_z[chunk][...].reshape(rows, WIDTHS[chunk])).astype(BF16)
        send_x[chunk][...] = moved.reshape(nxc, nz * 2, WIDTHS[chunk])

        @pl.loop(1, nxc)
        def _(step):
            x_copy(chunk, lax.rem(xc + step, nxc)).start()

        recv_x[chunk][xc] = send_x[chunk][xc]

    send_halo(0)
    start_z(0)
    start_z(1)

    for sweep in range(SWEEPS):
        through = matvec(diag_ref, val[...])
        resid = rhs_ref[...] - (through - coupled(sweep))
        val[...] = val[...] + matvec(prec_ref, resid)
        fill_halo(sweep + 1)
        send_halo(sweep + 1)
    sol_ref[...] = val[...]
    through = matvec(diag_ref, val[...])
    resid = rhs_ref[...] - (through - coupled(SWEEPS))
    both = mm(rmat, resid.astype(BF16))
    coarse[pl.ds(RHS_COL, 32), :] = both[:32] + both[32:]
    pack(2)
    start_z(2)

    forward(0)
    agg_rows = lax.broadcasted_iota(jnp.int32, (64, 128), 0)
    stay = jnp.where((agg_rows == slot_ref[...]) & (lane < 32), 1.0, 0.0).astype(BF16)
    stay_hi, stay_lo = halves(coarse[...])
    staying = nt(stay, stay_hi) + nt(stay, stay_lo)
    forward(1)
    forward(2)

    for chunk in (2, 0, 1):
        @pl.loop(1, nxc)
        def _(step):
            x_arrival(chunk, lax.rem(xc + step, nxc)).wait_recv()

        table = recv_x[chunk][...].reshape(rows, WIDTHS[chunk])
        if chunk == 2:
            want = lax.broadcasted_iota(jnp.int32, (8, 128), 1) == SLOT_COL - STARTS[2]
            slots = nt(jnp.where(want, 1.0, 0.0).astype(BF16), table)[:1]
            agg = lax.broadcasted_iota(jnp.int32, (64, rows), 0)
            gather = jnp.where(agg == slots.astype(jnp.int32), 1.0, 0.0).astype(BF16)
        begin, width = STARTS[chunk], WIDTHS[chunk]
        total = mm(gather, table) + staying[:, begin : begin + width]
        if chunk == 2:
            op_ref[:, pl.ds(begin, 89)] = total[:, :89]
            place = RHS_COL - begin
            crhs_ref[...] = total.T[place : place + 27]
        else:
            op_ref[:, pl.ds(begin, width)] = total

    for chunk in range(3):
        @pl.loop(1, nz)
        def _(step):
            z_copy(chunk, lax.rem(z + step, nz)).wait_send()

        @pl.loop(1, nxc)
        def _(step):
            x_copy(chunk, lax.rem(xc + step, nxc)).wait_send()

    for turn_no in range(SWEEPS + 1):
        for side in range(2):
            halo_copy(turn_no, side).wait_send()


def per_device(sizes, start, rhs, diag_block, precond, lift, neighbour, orient, owner, slot):
    nz, nxc, ny = sizes
    vmem = pl.BlockSpec(memory_space=pltpu.VMEM)
    lift_wide = jnp.pad(lift, ((0, 0), (0, 0), (0, 64)))
    rmat = jnp.asarray(split_restrict()).astype(BF16)
    scratch = [
        pltpu.VMEM((48, 32, 128), F32),
        pltpu.VMEM((COLS, 128), F32),
        pltpu.VMEM((64, 128), F32),
        pltpu.VMEM((128, 128), F32),
        pltpu.VMEM((128, 128), F32),
        pltpu.VMEM((8, 128), jnp.int32),
        pltpu.VMEM((8, 128), jnp.int32),
        pltpu.VMEM((SWEEPS + 1, 16, 128), F32),
        pltpu.VMEM((SWEEPS + 1, 2, 16, 128), F32),
        pltpu.VMEM((64, 128), F32),
    ]
    for blocks, depth in ((nz, nxc * 2), (nz, nxc * 2), (nxc, nz * 2), (nxc, nz * 2)):
        scratch += [pltpu.VMEM((blocks, depth, width), BF16) for width in WIDTHS]
    scratch += [
        pltpu.SemaphoreType.DMA((3, nz)),
        pltpu.SemaphoreType.DMA((3, nz)),
        pltpu.SemaphoreType.DMA((3, nxc)),
        pltpu.SemaphoreType.DMA((3, nxc)),
        pltpu.SemaphoreType.DMA((SWEEPS + 1, 2)),
        pltpu.SemaphoreType.DMA((SWEEPS + 1, 2)),
    ]
    sol, op, crhs = pl.pallas_call(
        functools.partial(kernel, nz, nxc, ny),
        out_shape=(
            jax.ShapeDtypeStruct((64, 128), F32),
            jax.ShapeDtypeStruct((64, 729), F32),
            jax.ShapeDtypeStruct((27, 64), F32),
        ),
        in_specs=[vmem] * 10,
        out_specs=(vmem, vmem, vmem),
        scratch_shapes=scratch,
        compiler_params=pltpu.CompilerParams(
            collective_id=0, has_side_effects=True, vmem_limit_bytes=48 * 1024 * 1024
        ),
    )(
        start,
        rhs,
        diag_block,
        precond,
        lift_wide,
        neighbour,
        orient,
        owner.reshape(1, -1),
        slot.reshape(1, -1),
        rmat,
    )
    return (sol, op.T, crhs)


def solution(mesh):
    sizes = (mesh.shape["dom"] // 8, 8, mesh.shape["face"])
    return jax.shard_map(
        functools.partial(per_device, sizes),
        mesh=mesh,
        in_specs=(
            P(None, ("dom", "face")),
            P(None, ("dom", "face")),
            P(None, None, ("dom", "face")),
            P(None, None, ("dom", "face")),
            P(),
            P(None, ("dom", "face")),
            P(None, ("dom", "face")),
            P(("dom", "face")),
            P(("dom", "face")),
        ),
        out_specs=(P(None, ("dom", "face")), P(None, ("dom", "face")), P(None, ("dom", "face"))),
        check_vma=False,
    )
```

```python
import functools

import jax
import jax.numpy as jnp
import numpy as np
from jax import lax
from jax.experimental import pallas as pl
from jax.experimental.pallas import tpu as pltpu
from jax.sharding import PartitionSpec as P

SWEEPS = 2
MESH = pl.DeviceIdType.MESH
WIDTHS = (384, 256, 128)
STARTS = (0, 384, 640)
COLS = 768
SLOT_COL = 383
RHS_COL = 736
F32 = jnp.float32
BF16 = jnp.bfloat16


def line_basis():
    fine_nodes = np.array([-1.0, -1.0 / np.sqrt(5.0), 1.0 / np.sqrt(5.0), 1.0])
    coarse_nodes = np.array([-1.0, 0.0, 1.0])
    basis = np.ones((4, 3))
    for column in range(3):
        for other in range(3):
            if other != column:
                basis[:, column] *= (fine_nodes - coarse_nodes[other]) / (
                    coarse_nodes[column] - coarse_nodes[other]
                )
    return basis


def restrict_table():
    basis = line_basis()
    prolong = (
        basis[:, None, None, :, None, None]
        * basis[None, :, None, None, :, None]
        * basis[None, None, :, None, None, :]
    ).reshape(64, 27)
    return prolong.T.astype(np.float32)


def split_restrict():
    table = restrict_table()
    high = table.astype(BF16).astype(np.float32)
    both = np.zeros((64, 64), np.float32)
    both[:27] = high
    both[32:59] = table - high
    return both


def nt(lhs, rhs):
    return lax.dot_general(lhs, rhs, (((1,), (1,)), ((), ())), preferred_element_type=F32)


def mm(lhs, rhs):
    return jnp.dot(lhs, rhs, preferred_element_type=F32)


def halves(value):
    high = value.astype(BF16)
    return high, (value - high.astype(F32)).astype(BF16)


def reduce_line(v0, v1, v2, v3):
    basis = line_basis()
    outs = []
    for column in range(3):
        total = None
        for value, weight in zip((v0, v1, v2, v3), basis[:, column]):
            if weight == 0.0:
                continue
            term = value if weight == 1.0 else value * np.float32(weight)
            total = term if total is None else total + term
        outs.append(total)
    return outs


def one_hot(mask):
    return jnp.where(mask, 1.0, 0.0).astype(BF16)


def kernel(
    nz,
    nxc,
    ny,
    start_hbm,
    rhs_hbm,
    diag_hbm,
    prec_hbm,
    lift_hbm,
    nb_hbm,
    ori_hbm,
    own_hbm,
    slot_hbm,
    rmat_hbm,
    sol_ref,
    op_ref,
    crhs_ref,
    val,
    rhs_ref,
    diag_ref,
    prec_ref,
    lift_ref,
    nb_ref,
    ori_ref,
    own_ref,
    slot_ref,
    rmat_ref,
    line,
    coarse,
    trace,
    lift_t,
    index,
    turn,
    halo_out,
    halo_in,
    product,
    pick_x,
    move_zx,
    move_xz,
    send_z0,
    send_z1,
    send_z2,
    recv_z0,
    recv_z1,
    recv_z2,
    send_x0,
    send_x1,
    send_x2,
    recv_x0,
    recv_x1,
    recv_x2,
    in_sem,
    zs_sem,
    zr_sem,
    xs_sem,
    xr_sem,
    hs_sem,
    hr_sem,
    near_sem,
    far_sem,
):
    send_z = (send_z0, send_z1, send_z2)
    recv_z = (recv_z0, recv_z1, recv_z2)
    send_x = (send_x0, send_x1, send_x2)
    recv_x = (recv_x0, recv_x1, recv_x2)
    dom = lax.axis_index("dom")
    y = lax.axis_index("face")
    z = lax.div(dom, nxc)
    xc = lax.rem(dom, nxc)
    above = lax.rem(y + 1, ny)
    below = lax.rem(y + ny - 1, ny)
    rows = nz * nxc * 2

    def at_z(shift):
        return (lax.rem(z + shift + nz, nz) * nxc + xc, y)

    barrier = pltpu.get_barrier_semaphore()
    for other in (above, below):
        pl.semaphore_signal(barrier, inc=1, device_id=(dom, other), device_id_type=MESH)
    for shift in (1, -1, 2, -2):
        pl.semaphore_signal(barrier, inc=1, device_id=at_z(shift), device_id_type=MESH)

    @pl.loop(1, nxc)
    def _(step):
        pl.semaphore_signal(
            barrier,
            inc=1,
            device_id=(z * nxc + lax.rem(xc + step, nxc), y),
            device_id_type=MESH,
        )

    pairs = [
        (start_hbm, val),
        (rmat_hbm, rmat_ref),
        (own_hbm, own_ref),
        (slot_hbm, slot_ref),
        (nb_hbm, nb_ref),
        (ori_hbm, ori_ref),
        (lift_hbm, lift_ref),
        (rhs_hbm, rhs_ref),
        (prec_hbm, prec_ref),
    ]
    fetches = [
        pltpu.make_async_copy(src, dst, in_sem.at[place])
        for place, (src, dst) in enumerate(pairs)
    ]
    slabs = [
        pltpu.make_async_copy(
            diag_hbm.at[pl.ds(16 * i, 16)], diag_ref.at[pl.ds(16 * i, 16)], in_sem.at[9 + i]
        )
        for i in range(4)
    ]
    for fetch in fetches[:4] + slabs + fetches[4:]:
        fetch.start()

    lane = lax.broadcasted_iota(jnp.int32, (1, 128), 1)

    def halo_copy(turn_no, side):
        return pltpu.make_async_remote_copy(
            src_ref=halo_out.at[turn_no, side],
            dst_ref=halo_in.at[turn_no, side],
            send_sem=hs_sem.at[turn_no],
            recv_sem=hr_sem.at[turn_no],
            device_id=(dom, above if side == 0 else below),
            device_id_type=MESH,
        )

    def halo_both(turn_no):
        return pltpu.make_async_remote_copy(
            src_ref=halo_out.at[turn_no],
            dst_ref=halo_in.at[turn_no],
            send_sem=hs_sem.at[turn_no],
            recv_sem=hr_sem.at[turn_no],
            device_id=(dom, above),
            device_id_type=MESH,
        )

    def send_halo(turn_no):
        low = jnp.concatenate([val[pl.ds(16 * i, 4), :] for i in range(4)], 0)
        high = jnp.concatenate([val[pl.ds(16 * i + 12, 4), :] for i in range(4)], 0)
        halo_out[turn_no, 0] = pltpu.roll(high, 32, 1)
        halo_out[turn_no, 1] = pltpu.roll(low, 96, 1)

    fetches[0].wait()
    send_halo(0)

    pl.semaphore_wait(barrier, 2 + 4 + nxc - 1)
    for side in range(2):
        halo_copy(0, side).start()
    if nz > 4:
        for side, shift in enumerate((2, -2)):
            pl.semaphore_signal(
                near_sem.at[side], inc=1, device_id=at_z(shift), device_id_type=MESH
            )

    coarse[pl.ds(728, 40), :] = jnp.zeros((40, 128), F32)
    for fetch in fetches[1:4]:
        fetch.wait()
    rmat = rmat_ref[...]
    for i in range(4):
        slabs[i].wait()
        planes = [[], [], []]
        for j in range(4):
            quad = []
            for k in range(4):
                both = mm(rmat, diag_ref[16 * i + 4 * j + k])
                quad.append(both[:32] + both[32:])
            for c, value in enumerate(reduce_line(*quad)):
                planes[c].append(value)
        for c in range(3):
            for b, value in enumerate(reduce_line(*planes[c])):
                line[9 * i + 3 * b + c] = value
    for bc in range(9):
        for a, value in enumerate(reduce_line(*[line[9 * i + bc] for i in range(4)])):
            place = 27 * (9 * a + bc)
            if place > SLOT_COL:
                coarse[pl.ds(place + 1, 27), :] = value[:27]
            elif place + 27 <= SLOT_COL:
                coarse[pl.ds(place, 27), :] = value[:27]
            else:
                head = SLOT_COL - place
                coarse[pl.ds(place, head), :] = value[:head]
                coarse[pl.ds(SLOT_COL + 1, 27 - head), :] = value[head:27]
    coarse[pl.ds(SLOT_COL, 1), :] = slot_ref[...].astype(F32)

    own = own_ref[...]
    own_cols = jnp.broadcast_to(own, (128, 128))
    own_rows = own_cols.T
    row_id = lax.broadcasted_iota(jnp.int32, (128, 128), 0)
    col_id = lax.broadcasted_iota(jnp.int32, (128, 128), 1)
    same = (own_rows == own_cols) & (row_id >= 32) & (row_id < col_id)
    rank = jnp.sum(jnp.where(same, 1.0, 0.0), axis=0, keepdims=True)
    key = jnp.where(lane >= 32, own * 2 + rank.astype(jnp.int32), -1)
    out_rows = lax.broadcasted_iota(jnp.int32, (rows, 128), 0)
    pick_z = one_hot(out_rows == key)

    def columns(chunk):
        return coarse[pl.ds(STARTS[chunk], WIDTHS[chunk]), :].astype(BF16)

    for chunk in (0, 1):
        packed = nt(pick_z, columns(chunk)).astype(BF16)
        send_z[chunk][...] = packed.reshape(nz, nxc * 2, WIDTHS[chunk])

    def z_copy(chunk, shift):
        other = lax.rem(z + shift + nz, nz)
        return pltpu.make_async_remote_copy(
            src_ref=send_z[chunk].at[other],
            dst_ref=recv_z[chunk].at[z],
            send_sem=zs_sem.at[chunk],
            recv_sem=zr_sem.at[chunk],
            device_id=(other * nxc + xc, y),
            device_id_type=MESH,
        )

    def z_all(chunk):
        return pltpu.make_async_remote_copy(
            src_ref=send_z[chunk].at[pl.ds(0, nz - 1)],
            dst_ref=recv_z[chunk].at[pl.ds(0, nz - 1)],
            send_sem=zs_sem.at[chunk],
            recv_sem=zr_sem.at[chunk],
            device_id=at_z(1),
            device_id_type=MESH,
        )

    def x_copy(chunk, step):
        other = lax.rem(xc + step, nxc)
        return pltpu.make_async_remote_copy(
            src_ref=send_x[chunk].at[other],
            dst_ref=recv_x[chunk].at[xc],
            send_sem=xs_sem.at[chunk],
            recv_sem=xr_sem.at[chunk],
            device_id=(z * nxc + other, y),
            device_id_type=MESH,
        )

    def x_all(chunk):
        return pltpu.make_async_remote_copy(
            src_ref=send_x[chunk].at[pl.ds(0, nxc - 1)],
            dst_ref=recv_x[chunk].at[pl.ds(0, nxc - 1)],
            send_sem=xs_sem.at[chunk],
            recv_sem=xr_sem.at[chunk],
            device_id=(z * nxc + lax.rem(xc + 1, nxc), y),
            device_id_type=MESH,
        )

    def z_pair(chunk, shift):
        z_copy(chunk, shift).start()
        if 2 * shift != nz:
            z_copy(chunk, -shift).start()

    def start_x(chunk):
        @pl.loop(1, nxc)
        def _(step):
            x_copy(chunk, step).start()

        recv_x[chunk][xc] = send_x[chunk][xc]

    half = nz // 2
    for chunk in (0, 1):
        for shift in range(1, min(2, half) + 1):
            z_pair(chunk, shift)
    if nz > 4:
        for side in range(2):
            pl.semaphore_wait(near_sem.at[side], 1)
        if nz > 8:
            for side, shift in enumerate((4, -4)):
                pl.semaphore_signal(
                    far_sem.at[side], inc=1, device_id=at_z(shift), device_id_type=MESH
                )
        for chunk in (0, 1):
            for shift in range(3, min(4, half) + 1):
                z_pair(chunk, shift)
    for chunk in (0, 1):
        recv_z[chunk][z] = send_z[chunk][z]

    for fetch in fetches[4:7]:
        fetch.wait()
    trace[...] = jnp.zeros((128, 128), F32)
    lift_t[...] = jnp.zeros((128, 128), F32)
    for f in range(6):
        lift_t[pl.ds(f, 16, stride=8), :] = jnp.concatenate(
            [lift_ref[f], jnp.zeros((16, 64), F32)], 1
        )
    lift_hi, lift_lo = halves(lift_t[...].T[:64])
    index[...] = jnp.zeros((8, 128), jnp.int32)
    turn[...] = jnp.zeros((8, 128), jnp.int32)
    index[pl.ds(0, 6), :] = nb_ref[...] & 127
    turn[pl.ds(0, 6), :] = ori_ref[...]
    idx = index[...]
    flip_row = (turn[...] & 1) != 0
    flip_col = (turn[...] & 2) != 0
    swap = (turn[...] & 4) != 0
    face_id = lax.broadcasted_iota(jnp.int32, (8, 128), 0)
    lane8 = lax.broadcasted_iota(jnp.int32, (8, 128), 1)
    from_low = (face_id == 2) & (lane8 < 32)
    from_high = (face_id == 3) & (lane8 >= 96)

    def matvec(matrix_ref, vector):
        for block in range(8):
            part = matrix_ref[pl.ds(8 * block, 8)].astype(F32) * vector[None]
            product[pl.ds(8 * block, 8), :] = jnp.sum(part, axis=1)
        return product[...]

    def coupled(turn_no):
        trace[pl.ds(1, 16, stride=8), :] = val[pl.ds(0, 16), :]
        trace[pl.ds(0, 16, stride=8), :] = val[pl.ds(48, 16), :]
        for i in range(4):
            trace[pl.ds(32 * i + 3, 4, stride=8), :] = val[pl.ds(16 * i, 4), :]
            trace[pl.ds(32 * i + 2, 4, stride=8), :] = val[pl.ds(16 * i + 12, 4), :]
        trace[pl.ds(5, 16, stride=8), :] = val[pl.ds(0, 16, stride=4), :]
        trace[pl.ds(4, 16, stride=8), :] = val[pl.ds(3, 16, stride=4), :]
        cells = [
            jnp.take_along_axis(
                trace[pl.ds(8 * k, 8), :], idx, axis=1, mode="promise_in_bounds"
            )
            for k in range(16)
        ]
        halo_both(turn_no).wait_recv()
        low = jnp.where(y > 0, halo_in[turn_no, 0], 0.0)
        high = jnp.where(y < ny - 1, halo_in[turn_no, 1], 0.0)
        cells = [jnp.where(from_low, low[k : k + 1], cells[k]) for k in range(16)]
        cells = [jnp.where(from_high, high[k : k + 1], cells[k]) for k in range(16)]
        cells = [jnp.where(swap, cells[4 * (k % 4) + k // 4], cells[k]) for k in range(16)]
        cells = [jnp.where(flip_row, cells[4 * (3 - k // 4) + k % 4], cells[k]) for k in range(16)]
        cells = [jnp.where(flip_col, cells[4 * (k // 4) + 3 - k % 4], cells[k]) for k in range(16)]
        turned_hi, turned_lo = halves(jnp.concatenate(cells, 0))
        return mm(lift_hi, turned_hi) + (mm(lift_hi, turned_lo) + mm(lift_lo, turned_hi))

    fetches[7].wait()
    for sweep in range(SWEEPS):
        through = rhs_ref[...] - matvec(diag_ref, val[...])
        resid = through + coupled(sweep)
        if sweep == 0:
            fetches[8].wait()
        val[...] = val[...] + matvec(prec_ref, resid)
        send_halo(sweep + 1)
        for side in range(2):
            halo_copy(sweep + 1, side).start()
        if sweep == 0:
            if nz > 8:
                for side in range(2):
                    pl.semaphore_wait(far_sem.at[side], 1)
                for chunk in (0, 1):
                    for shift in range(half, 4, -1):
                        z_pair(chunk, shift)
            s = lax.broadcasted_iota(jnp.int32, (rows, 128), 0)
            deep = 2 * nz
            wide = 2 * nxc
            target = (((s & (deep - 1)) >> 1) * wide) + ((s // deep) * 2) + (s & 1)
            pick_x[...] = one_hot(target == key)
            s = lax.broadcasted_iota(jnp.int32, (rows, rows), 0)
            q = lax.broadcasted_iota(jnp.int32, (rows, rows), 1)
            target = (((s & (deep - 1)) >> 1) * wide) + ((s // deep) * 2) + (s & 1)
            move_zx[...] = one_hot(q == target)
            target = (((s & (wide - 1)) >> 1) * deep) + ((s // wide) * 2) + (s & 1)
            move_xz[...] = one_hot(q == target)
    sol_ref[...] = val[...]
    through = rhs_ref[...] - matvec(diag_ref, val[...])
    resid = through + coupled(SWEEPS)
    both = mm(rmat, resid.astype(BF16))
    coarse[pl.ds(RHS_COL, 32), :] = both[:32] + both[32:]
    packed = nt(pick_x[...], columns(2)).astype(BF16)
    send_x[2][...] = packed.reshape(nxc, nz * 2, WIDTHS[2])
    start_x(2)

    def forward(chunk):
        z_all(chunk).wait_recv()
        table = recv_z[chunk][...].reshape(rows, WIDTHS[chunk])
        moved = mm(move_zx[...], table).astype(BF16)
        send_x[chunk][...] = moved.reshape(nxc, nz * 2, WIDTHS[chunk])
        start_x(chunk)

    forward(0)
    agg_rows = lax.broadcasted_iota(jnp.int32, (64, 128), 0)
    stay = one_hot((agg_rows == slot_ref[...]) & (lane < 32))
    stay_hi, stay_lo = halves(coarse[...])
    staying = nt(stay, stay_hi) + nt(stay, stay_lo)

    x_all(2).wait_recv()
    moved = mm(move_xz[...], recv_x[2][...].reshape(rows, WIDTHS[2])).astype(BF16)
    send_z[2][...] = moved.reshape(nz, nxc * 2, WIDTHS[2])
    for shift in range(half, 0, -1):
        z_pair(2, shift)
    recv_z[2][z] = send_z[2][z]

    forward(1)
    x_all(0).wait_recv()
    table = recv_x[0][...].reshape(rows, WIDTHS[0])
    want = lax.broadcasted_iota(jnp.int32, (8, WIDTHS[0]), 1) == SLOT_COL
    slots = nt(one_hot(want), table)[:1]
    agg = lax.broadcasted_iota(jnp.int32, (64, rows), 0)
    gather = one_hot(agg == slots.astype(jnp.int32))
    gather_zx = mm(gather, move_zx[...]).astype(BF16)
    total = mm(gather, table) + staying[:, : WIDTHS[0]]
    op_ref[:, pl.ds(0, SLOT_COL)] = total[:, :SLOT_COL]
    x_all(1).wait_recv()
    table = recv_x[1][...].reshape(rows, WIDTHS[1])
    total = mm(gather, table) + staying[:, STARTS[1] : STARTS[2]]
    op_ref[:, pl.ds(SLOT_COL, WIDTHS[1])] = total

    for chunk in range(3):
        z_all(chunk).wait_send()
        x_all(chunk).wait_send()
    for turn_no in range(SWEEPS + 1):
        halo_both(turn_no).wait_send()

    z_all(2).wait_recv()
    table = recv_z[2][...].reshape(rows, WIDTHS[2])
    total = mm(gather_zx, table) + staying[:, STARTS[2] :]
    tail = 729 - SLOT_COL - WIDTHS[1]
    op_ref[:, pl.ds(729 - tail, tail)] = total[:, :tail]
    place = RHS_COL - STARTS[2]
    crhs_ref[...] = total.T[place : place + 27]


def per_device(sizes, start, rhs, diag_block, precond, lift, neighbour, orient, owner, slot):
    nz, nxc, ny = sizes
    rows = nz * nxc * 2
    vmem = pl.BlockSpec(memory_space=pltpu.VMEM)
    anywhere = pl.BlockSpec(memory_space=pl.ANY)
    rmat = jnp.asarray(split_restrict().astype(BF16))
    scratch = [
        pltpu.VMEM((64, 128), F32),
        pltpu.VMEM((64, 128), F32),
        pltpu.VMEM((64, 64, 128), BF16),
        pltpu.VMEM((64, 64, 128), BF16),
        pltpu.VMEM((6, 16, 64), F32),
        pltpu.VMEM((6, 128), jnp.int32),
        pltpu.VMEM((6, 128), jnp.int32),
        pltpu.VMEM((1, 128), jnp.int32),
        pltpu.VMEM((1, 128), jnp.int32),
        pltpu.VMEM((64, 64), BF16),
        pltpu.VMEM((36, 32, 128), F32),
        pltpu.VMEM((COLS, 128), F32),
        pltpu.VMEM((128, 128), F32),
        pltpu.VMEM((128, 128), F32),
        pltpu.VMEM((8, 128), jnp.int32),
        pltpu.VMEM((8, 128), jnp.int32),
        pltpu.VMEM((SWEEPS + 1, 2, 16, 128), F32),
        pltpu.VMEM((SWEEPS + 1, 2, 16, 128), F32),
        pltpu.VMEM((64, 128), F32),
        pltpu.VMEM((rows, 128), BF16),
        pltpu.VMEM((rows, rows), BF16),
        pltpu.VMEM((rows, rows), BF16),
    ]
    for blocks, depth in ((nz, nxc * 2), (nz, nxc * 2), (nxc, nz * 2), (nxc, nz * 2)):
        scratch += [pltpu.VMEM((blocks, depth, width), BF16) for width in WIDTHS]
    scratch += [
        pltpu.SemaphoreType.DMA((13,)),
        pltpu.SemaphoreType.DMA((3,)),
        pltpu.SemaphoreType.DMA((3,)),
        pltpu.SemaphoreType.DMA((3,)),
        pltpu.SemaphoreType.DMA((3,)),
        pltpu.SemaphoreType.DMA((SWEEPS + 1,)),
        pltpu.SemaphoreType.DMA((SWEEPS + 1,)),
        pltpu.SemaphoreType.REGULAR((2,)),
        pltpu.SemaphoreType.REGULAR((2,)),
    ]
    sol, op, crhs = pl.pallas_call(
        functools.partial(kernel, nz, nxc, ny),
        out_shape=(
            jax.ShapeDtypeStruct((64, 128), F32),
            jax.ShapeDtypeStruct((64, 729), F32),
            jax.ShapeDtypeStruct((27, 64), F32),
        ),
        in_specs=[anywhere] * 10,
        out_specs=(vmem, vmem, vmem),
        scratch_shapes=scratch,
        compiler_params=pltpu.CompilerParams(
            collective_id=0, has_side_effects=True, vmem_limit_bytes=60 * 1024 * 1024
        ),
    )(
        start,
        rhs,
        diag_block,
        precond,
        lift,
        neighbour,
        orient,
        owner.reshape(1, -1),
        slot.reshape(1, -1),
        rmat,
    )
    return (sol, op.T, crhs)


def solution(mesh):
    sizes = (mesh.shape["dom"] // 8, 8, mesh.shape["face"])
    return jax.shard_map(
        functools.partial(per_device, sizes),
        mesh=mesh,
        in_specs=(
            P(None, ("dom", "face")),
            P(None, ("dom", "face")),
            P(None, None, ("dom", "face")),
            P(None, None, ("dom", "face")),
            P(),
            P(None, ("dom", "face")),
            P(None, ("dom", "face")),
            P(("dom", "face")),
            P(("dom", "face")),
        ),
        out_specs=(P(None, ("dom", "face")), P(None, ("dom", "face")), P(None, ("dom", "face"))),
        check_vma=False,
    )
```

```python
import functools

import jax
import jax.numpy as jnp
import numpy as np
from jax import lax
from jax.experimental import pallas as pl
from jax.experimental.pallas import tpu as pltpu
from jax.sharding import PartitionSpec as P

SWEEPS = 2
MESH = pl.DeviceIdType.MESH
WIDTHS = (384, 256, 128)
STARTS = (0, 384, 640)
COLS = 768
SLOT_COL = 383
RHS_COL = 736
F32 = jnp.float32
BF16 = jnp.bfloat16


def line_basis():
    fine_nodes = np.array([-1.0, -1.0 / np.sqrt(5.0), 1.0 / np.sqrt(5.0), 1.0])
    coarse_nodes = np.array([-1.0, 0.0, 1.0])
    basis = np.ones((4, 3))
    for column in range(3):
        for other in range(3):
            if other != column:
                basis[:, column] *= (fine_nodes - coarse_nodes[other]) / (
                    coarse_nodes[column] - coarse_nodes[other]
                )
    return basis


def restrict_table():
    basis = line_basis()
    prolong = (
        basis[:, None, None, :, None, None]
        * basis[None, :, None, None, :, None]
        * basis[None, None, :, None, None, :]
    ).reshape(64, 27)
    return prolong.T.astype(np.float32)


def split_restrict():
    table = restrict_table()
    high = table.astype(BF16).astype(np.float32)
    both = np.zeros((64, 64), np.float32)
    both[:27] = high
    both[32:59] = table - high
    return both


def nt(lhs, rhs):
    return lax.dot_general(lhs, rhs, (((1,), (1,)), ((), ())), preferred_element_type=F32)


def mm(lhs, rhs):
    return jnp.dot(lhs, rhs, preferred_element_type=F32)


def halves(value):
    high = value.astype(BF16)
    return high, (value - high.astype(F32)).astype(BF16)


def reduce_line(v0, v1, v2, v3):
    basis = line_basis()
    outs = []
    for column in range(3):
        total = None
        for value, weight in zip((v0, v1, v2, v3), basis[:, column]):
            if weight == 0.0:
                continue
            term = value if weight == 1.0 else value * np.float32(weight)
            total = term if total is None else total + term
        outs.append(total)
    return outs


def one_hot(mask):
    return jnp.where(mask, 1.0, 0.0).astype(BF16)


def kernel(
    nz,
    nxc,
    ny,
    start_hbm,
    rhs_hbm,
    diag_hbm,
    prec_hbm,
    lift_hbm,
    nb_hbm,
    ori_hbm,
    own_hbm,
    slot_hbm,
    rmat_hbm,
    sol_ref,
    op_ref,
    crhs_ref,
    val,
    rhs_ref,
    diag_ref,
    prec_ref,
    lift_ref,
    nb_ref,
    ori_ref,
    own_ref,
    slot_ref,
    rmat_ref,
    line,
    coarse,
    trace,
    lift_t,
    index,
    turn,
    halo_out,
    halo_in,
    product,
    pick_x,
    move_zx,
    move_xz,
    send_z0,
    send_z1,
    send_z2,
    recv_z0,
    recv_z1,
    recv_z2,
    send_x0,
    send_x1,
    send_x2,
    recv_x0,
    recv_x1,
    recv_x2,
    in_sem,
    zs_sem,
    zr_sem,
    xs_sem,
    xr_sem,
    hs_sem,
    hr_sem,
    near_sem,
    far_sem,
):
    send_z = (send_z0, send_z1, send_z2)
    recv_z = (recv_z0, recv_z1, recv_z2)
    send_x = (send_x0, send_x1, send_x2)
    recv_x = (recv_x0, recv_x1, recv_x2)
    dom = lax.axis_index("dom")
    y = lax.axis_index("face")
    z = lax.div(dom, nxc)
    xc = lax.rem(dom, nxc)
    above = lax.rem(y + 1, ny)
    below = lax.rem(y + ny - 1, ny)
    rows = nz * nxc * 2

    def at_z(shift):
        return (lax.rem(z + shift + nz, nz) * nxc + xc, y)

    barrier = pltpu.get_barrier_semaphore()
    for other in (above, below):
        pl.semaphore_signal(barrier, inc=1, device_id=(dom, other), device_id_type=MESH)
    for shift in (1, -1, 2, -2):
        pl.semaphore_signal(barrier, inc=1, device_id=at_z(shift), device_id_type=MESH)

    @pl.loop(1, nxc)
    def _(step):
        pl.semaphore_signal(
            barrier,
            inc=1,
            device_id=(z * nxc + lax.rem(xc + step, nxc), y),
            device_id_type=MESH,
        )

    pairs = [
        (start_hbm, val),
        (rmat_hbm, rmat_ref),
        (own_hbm, own_ref),
        (slot_hbm, slot_ref),
        (nb_hbm, nb_ref),
        (ori_hbm, ori_ref),
        (lift_hbm, lift_ref),
        (rhs_hbm, rhs_ref),
        (prec_hbm, prec_ref),
    ]
    fetches = [
        pltpu.make_async_copy(src, dst, in_sem.at[place])
        for place, (src, dst) in enumerate(pairs)
    ]
    slabs = [
        pltpu.make_async_copy(
            diag_hbm.at[pl.ds(16 * i, 16)], diag_ref.at[pl.ds(16 * i, 16)], in_sem.at[9 + i]
        )
        for i in range(4)
    ]
    for fetch in fetches[:4] + slabs + fetches[4:]:
        fetch.start()

    lane = lax.broadcasted_iota(jnp.int32, (1, 128), 1)

    def halo_copy(turn_no, side):
        return pltpu.make_async_remote_copy(
            src_ref=halo_out.at[turn_no, side],
            dst_ref=halo_in.at[turn_no, side],
            send_sem=hs_sem.at[turn_no],
            recv_sem=hr_sem.at[turn_no],
            device_id=(dom, above if side == 0 else below),
            device_id_type=MESH,
        )

    def halo_both(turn_no):
        return pltpu.make_async_remote_copy(
            src_ref=halo_out.at[turn_no],
            dst_ref=halo_in.at[turn_no],
            send_sem=hs_sem.at[turn_no],
            recv_sem=hr_sem.at[turn_no],
            device_id=(dom, above),
            device_id_type=MESH,
        )

    def send_halo(turn_no):
        low = jnp.concatenate([val[pl.ds(16 * i, 4), :] for i in range(4)], 0)
        high = jnp.concatenate([val[pl.ds(16 * i + 12, 4), :] for i in range(4)], 0)
        halo_out[turn_no, 0] = pltpu.roll(high, 32, 1)
        halo_out[turn_no, 1] = pltpu.roll(low, 96, 1)

    fetches[0].wait()
    send_halo(0)

    pl.semaphore_wait(barrier, 2 + 4 + nxc - 1)
    for side in range(2):
        halo_copy(0, side).start()
    if nz > 4:
        for side, shift in enumerate((2, -2)):
            pl.semaphore_signal(
                near_sem.at[side], inc=1, device_id=at_z(shift), device_id_type=MESH
            )

    coarse[pl.ds(728, 40), :] = jnp.zeros((40, 128), F32)
    for fetch in fetches[1:4]:
        fetch.wait()
    rmat = rmat_ref[...]
    for i in range(4):
        slabs[i].wait()
        planes = [[], [], []]
        for j in range(4):
            quad = []
            for k in range(4):
                both = mm(rmat, diag_ref[16 * i + 4 * j + k])
                quad.append(both[:32] + both[32:])
            for c, value in enumerate(reduce_line(*quad)):
                planes[c].append(value)
        for c in range(3):
            for b, value in enumerate(reduce_line(*planes[c])):
                line[9 * i + 3 * b + c] = value
    for bc in range(9):
        for a, value in enumerate(reduce_line(*[line[9 * i + bc] for i in range(4)])):
            place = 27 * (9 * a + bc)
            if place > SLOT_COL:
                coarse[pl.ds(place + 1, 27), :] = value[:27]
            elif place + 27 <= SLOT_COL:
                coarse[pl.ds(place, 27), :] = value[:27]
            else:
                head = SLOT_COL - place
                coarse[pl.ds(place, head), :] = value[:head]
                coarse[pl.ds(SLOT_COL + 1, 27 - head), :] = value[head:27]
    coarse[pl.ds(SLOT_COL, 1), :] = slot_ref[...].astype(F32)

    own = own_ref[...]
    own_cols = jnp.broadcast_to(own, (128, 128))
    own_rows = own_cols.T
    row_id = lax.broadcasted_iota(jnp.int32, (128, 128), 0)
    col_id = lax.broadcasted_iota(jnp.int32, (128, 128), 1)
    same = (own_rows == own_cols) & (row_id >= 32) & (row_id < col_id)
    rank = jnp.sum(jnp.where(same, 1.0, 0.0), axis=0, keepdims=True)
    key = jnp.where(lane >= 32, own * 2 + rank.astype(jnp.int32), -1)
    out_rows = lax.broadcasted_iota(jnp.int32, (rows, 128), 0)
    pick_z = one_hot(out_rows == key)

    def columns(chunk):
        return coarse[pl.ds(STARTS[chunk], WIDTHS[chunk]), :].astype(BF16)

    packed = nt(pick_z, columns(0)).astype(BF16)
    send_z[0][...] = packed.reshape(nz, nxc * 2, WIDTHS[0])

    def z_copy(chunk, shift):
        other = lax.rem(z + shift + nz, nz)
        return pltpu.make_async_remote_copy(
            src_ref=send_z[chunk].at[other],
            dst_ref=recv_z[chunk].at[z],
            send_sem=zs_sem.at[chunk],
            recv_sem=zr_sem.at[chunk],
            device_id=(other * nxc + xc, y),
            device_id_type=MESH,
        )

    def z_all(chunk):
        return pltpu.make_async_remote_copy(
            src_ref=send_z[chunk].at[pl.ds(0, nz - 1)],
            dst_ref=recv_z[chunk].at[pl.ds(0, nz - 1)],
            send_sem=zs_sem.at[chunk],
            recv_sem=zr_sem.at[chunk],
            device_id=at_z(1),
            device_id_type=MESH,
        )

    def x_copy(chunk, step):
        other = lax.rem(xc + step, nxc)
        return pltpu.make_async_remote_copy(
            src_ref=send_x[chunk].at[other],
            dst_ref=recv_x[chunk].at[xc],
            send_sem=xs_sem.at[chunk],
            recv_sem=xr_sem.at[chunk],
            device_id=(z * nxc + other, y),
            device_id_type=MESH,
        )

    def x_all(chunk):
        return pltpu.make_async_remote_copy(
            src_ref=send_x[chunk].at[pl.ds(0, nxc - 1)],
            dst_ref=recv_x[chunk].at[pl.ds(0, nxc - 1)],
            send_sem=xs_sem.at[chunk],
            recv_sem=xr_sem.at[chunk],
            device_id=(z * nxc + lax.rem(xc + 1, nxc), y),
            device_id_type=MESH,
        )

    def z_pair(chunk, shift):
        z_copy(chunk, shift).start()
        if 2 * shift != nz:
            z_copy(chunk, -shift).start()

    def start_x(chunk):
        @pl.loop(1, nxc)
        def _(step):
            x_copy(chunk, step).start()

        recv_x[chunk][xc] = send_x[chunk][xc]

    def pack_x(chunk):
        packed = nt(pick_x[...], columns(chunk)).astype(BF16)
        send_x[chunk][...] = packed.reshape(nxc, nz * 2, WIDTHS[chunk])
        start_x(chunk)

    half = nz // 2
    for shift in range(1, min(2, half) + 1):
        z_pair(0, shift)
    s = lax.broadcasted_iota(jnp.int32, (rows, 128), 0)
    deep = 2 * nz
    wide = 2 * nxc
    target = (((s & (deep - 1)) >> 1) * wide) + ((s // deep) * 2) + (s & 1)
    pick_x[...] = one_hot(target == key)
    pack_x(1)
    if nz > 4:
        for side in range(2):
            pl.semaphore_wait(near_sem.at[side], 1)
        if nz > 8:
            for side, shift in enumerate((4, -4)):
                pl.semaphore_signal(
                    far_sem.at[side], inc=1, device_id=at_z(shift), device_id_type=MESH
                )
        for shift in range(3, min(4, half) + 1):
            z_pair(0, shift)
    recv_z[0][z] = send_z[0][z]

    s = lax.broadcasted_iota(jnp.int32, (rows, rows), 0)
    q = lax.broadcasted_iota(jnp.int32, (rows, rows), 1)
    target = (((s & (deep - 1)) >> 1) * wide) + ((s // deep) * 2) + (s & 1)
    move_zx[...] = one_hot(q == target)
    target = (((s & (wide - 1)) >> 1) * deep) + ((s // wide) * 2) + (s & 1)
    move_xz[...] = one_hot(q == target)

    def onward(chunk):
        x_all(chunk).wait_recv()
        table = recv_x[chunk][...].reshape(rows, WIDTHS[chunk])
        moved = mm(move_xz[...], table).astype(BF16)
        send_z[chunk][...] = moved.reshape(nz, nxc * 2, WIDTHS[chunk])
        recv_z[chunk][z] = send_z[chunk][z]

    for fetch in fetches[4:7]:
        fetch.wait()
    trace[...] = jnp.zeros((128, 128), F32)
    lift_t[...] = jnp.zeros((128, 128), F32)
    for f in range(6):
        lift_t[pl.ds(f, 16, stride=8), :] = jnp.concatenate(
            [lift_ref[f], jnp.zeros((16, 64), F32)], 1
        )
    lift_hi, lift_lo = halves(lift_t[...].T[:64])
    index[...] = jnp.zeros((8, 128), jnp.int32)
    turn[...] = jnp.zeros((8, 128), jnp.int32)
    index[pl.ds(0, 6), :] = nb_ref[...] & 127
    turn[pl.ds(0, 6), :] = ori_ref[...]
    idx = index[...]
    flip_row = (turn[...] & 1) != 0
    flip_col = (turn[...] & 2) != 0
    swap = (turn[...] & 4) != 0
    face_id = lax.broadcasted_iota(jnp.int32, (8, 128), 0)
    lane8 = lax.broadcasted_iota(jnp.int32, (8, 128), 1)
    from_low = (face_id == 2) & (lane8 < 32)
    from_high = (face_id == 3) & (lane8 >= 96)

    def matvec(matrix_ref, vector):
        for block in range(8):
            part = matrix_ref[pl.ds(8 * block, 8)].astype(F32) * vector[None]
            product[pl.ds(8 * block, 8), :] = jnp.sum(part, axis=1)
        return product[...]

    def coupled(turn_no):
        trace[pl.ds(1, 16, stride=8), :] = val[pl.ds(0, 16), :]
        trace[pl.ds(0, 16, stride=8), :] = val[pl.ds(48, 16), :]
        for i in range(4):
            trace[pl.ds(32 * i + 3, 4, stride=8), :] = val[pl.ds(16 * i, 4), :]
            trace[pl.ds(32 * i + 2, 4, stride=8), :] = val[pl.ds(16 * i + 12, 4), :]
        trace[pl.ds(5, 16, stride=8), :] = val[pl.ds(0, 16, stride=4), :]
        trace[pl.ds(4, 16, stride=8), :] = val[pl.ds(3, 16, stride=4), :]
        cells = [
            jnp.take_along_axis(
                trace[pl.ds(8 * k, 8), :], idx, axis=1, mode="promise_in_bounds"
            )
            for k in range(16)
        ]
        halo_both(turn_no).wait_recv()
        low = jnp.where(y > 0, halo_in[turn_no, 0], 0.0)
        high = jnp.where(y < ny - 1, halo_in[turn_no, 1], 0.0)
        cells = [jnp.where(from_low, low[k : k + 1], cells[k]) for k in range(16)]
        cells = [jnp.where(from_high, high[k : k + 1], cells[k]) for k in range(16)]
        cells = [jnp.where(swap, cells[4 * (k % 4) + k // 4], cells[k]) for k in range(16)]
        cells = [jnp.where(flip_row, cells[4 * (3 - k // 4) + k % 4], cells[k]) for k in range(16)]
        cells = [jnp.where(flip_col, cells[4 * (k // 4) + 3 - k % 4], cells[k]) for k in range(16)]
        turned_hi, turned_lo = halves(jnp.concatenate(cells, 0))
        return mm(lift_hi, turned_hi) + (mm(lift_hi, turned_lo) + mm(lift_lo, turned_hi))

    fetches[7].wait()
    for sweep in range(SWEEPS):
        through = rhs_ref[...] - matvec(diag_ref, val[...])
        resid = through + coupled(sweep)
        if sweep == 0:
            fetches[8].wait()
        val[...] = val[...] + matvec(prec_ref, resid)
        send_halo(sweep + 1)
        for side in range(2):
            halo_copy(sweep + 1, side).start()
        if sweep == 0:
            if nz > 8:
                for side in range(2):
                    pl.semaphore_wait(far_sem.at[side], 1)
                for shift in range(half, 4, -1):
                    z_pair(0, shift)
            onward(1)
            for shift in range(half, 0, -1):
                z_pair(1, shift)
    sol_ref[...] = val[...]
    through = rhs_ref[...] - matvec(diag_ref, val[...])
    resid = through + coupled(SWEEPS)
    both = mm(rmat, resid.astype(BF16))
    coarse[pl.ds(RHS_COL, 32), :] = both[:32] + both[32:]
    pack_x(2)

    z_all(0).wait_recv()
    table = recv_z[0][...].reshape(rows, WIDTHS[0])
    moved = mm(move_zx[...], table).astype(BF16)
    send_x[0][...] = moved.reshape(nxc, nz * 2, WIDTHS[0])
    start_x(0)

    agg_rows = lax.broadcasted_iota(jnp.int32, (64, 128), 0)
    stay = one_hot((agg_rows == slot_ref[...]) & (lane < 32))
    stay_hi, stay_lo = halves(coarse[...])
    staying = nt(stay, stay_hi) + nt(stay, stay_lo)

    onward(2)
    for shift in range(half, 0, -1):
        z_pair(2, shift)

    x_all(0).wait_recv()
    table = recv_x[0][...].reshape(rows, WIDTHS[0])
    want = lax.broadcasted_iota(jnp.int32, (8, WIDTHS[0]), 1) == SLOT_COL
    slots = nt(one_hot(want), table)[:1]
    agg = lax.broadcasted_iota(jnp.int32, (64, rows), 0)
    gather = one_hot(agg == slots.astype(jnp.int32))
    gather_zx = mm(gather, move_zx[...]).astype(BF16)
    total = mm(gather, table) + staying[:, : WIDTHS[0]]
    op_ref[:, pl.ds(0, SLOT_COL)] = total[:, :SLOT_COL]
    z_all(1).wait_recv()
    table = recv_z[1][...].reshape(rows, WIDTHS[1])
    total = mm(gather_zx, table) + staying[:, STARTS[1] : STARTS[2]]
    op_ref[:, pl.ds(SLOT_COL, WIDTHS[1])] = total

    for chunk in range(3):
        z_all(chunk).wait_send()
        x_all(chunk).wait_send()
    for turn_no in range(SWEEPS + 1):
        halo_both(turn_no).wait_send()

    z_all(2).wait_recv()
    table = recv_z[2][...].reshape(rows, WIDTHS[2])
    total = mm(gather_zx, table) + staying[:, STARTS[2] :]
    tail = 729 - SLOT_COL - WIDTHS[1]
    op_ref[:, pl.ds(729 - tail, tail)] = total[:, :tail]
    place = RHS_COL - STARTS[2]
    crhs_ref[...] = total.T[place : place + 27]


def hand_over(sol_in, op_in, crhs_in, sol_ref, op_ref, crhs_ref):
    sol_ref[...] = sol_in[...]
    op_ref[...] = op_in[...]
    crhs_ref[...] = crhs_in[...]


def per_device(sizes, start, rhs, diag_block, precond, lift, neighbour, orient, owner, slot):
    nz, nxc, ny = sizes
    rows = nz * nxc * 2
    vmem = pl.BlockSpec(memory_space=pltpu.VMEM)
    anywhere = pl.BlockSpec(memory_space=pltpu.HBM)
    rmat = jnp.asarray(split_restrict().astype(BF16))
    scratch = [
        pltpu.VMEM((64, 128), F32),
        pltpu.VMEM((64, 128), F32),
        pltpu.VMEM((64, 64, 128), BF16),
        pltpu.VMEM((64, 64, 128), BF16),
        pltpu.VMEM((6, 16, 64), F32),
        pltpu.VMEM((6, 128), jnp.int32),
        pltpu.VMEM((6, 128), jnp.int32),
        pltpu.VMEM((1, 128), jnp.int32),
        pltpu.VMEM((1, 128), jnp.int32),
        pltpu.VMEM((64, 64), BF16),
        pltpu.VMEM((36, 32, 128), F32),
        pltpu.VMEM((COLS, 128), F32),
        pltpu.VMEM((128, 128), F32),
        pltpu.VMEM((128, 128), F32),
        pltpu.VMEM((8, 128), jnp.int32),
        pltpu.VMEM((8, 128), jnp.int32),
        pltpu.VMEM((SWEEPS + 1, 2, 16, 128), F32),
        pltpu.VMEM((SWEEPS + 1, 2, 16, 128), F32),
        pltpu.VMEM((64, 128), F32),
        pltpu.VMEM((rows, 128), BF16),
        pltpu.VMEM((rows, rows), BF16),
        pltpu.VMEM((rows, rows), BF16),
    ]
    for blocks, depth in ((nz, nxc * 2), (nz, nxc * 2), (nxc, nz * 2), (nxc, nz * 2)):
        scratch += [pltpu.VMEM((blocks, depth, width), BF16) for width in WIDTHS]
    scratch += [
        pltpu.SemaphoreType.DMA((13,)),
        pltpu.SemaphoreType.DMA((3,)),
        pltpu.SemaphoreType.DMA((3,)),
        pltpu.SemaphoreType.DMA((3,)),
        pltpu.SemaphoreType.DMA((3,)),
        pltpu.SemaphoreType.DMA((SWEEPS + 1,)),
        pltpu.SemaphoreType.DMA((SWEEPS + 1,)),
        pltpu.SemaphoreType.REGULAR((2,)),
        pltpu.SemaphoreType.REGULAR((2,)),
    ]
    parts = pl.pallas_call(
        functools.partial(kernel, nz, nxc, ny),
        out_shape=(
            jax.ShapeDtypeStruct((64, 128), F32),
            jax.ShapeDtypeStruct((64, 729), F32),
            jax.ShapeDtypeStruct((27, 64), F32),
        ),
        in_specs=[anywhere] * 10,
        out_specs=(vmem, vmem, vmem),
        scratch_shapes=scratch,
        compiler_params=pltpu.CompilerParams(
            collective_id=0, has_side_effects=True, vmem_limit_bytes=60 * 1024 * 1024
        ),
    )(
        start,
        rhs,
        diag_block,
        precond,
        lift,
        neighbour,
        orient,
        owner.reshape(1, -1),
        slot.reshape(1, -1),
        rmat,
    )
    sol, op, crhs = pl.pallas_call(
        hand_over,
        out_shape=tuple(jax.ShapeDtypeStruct(part.shape, F32) for part in parts),
        in_specs=[vmem] * 3,
        out_specs=(vmem, vmem, vmem),
    )(*parts)
    return (sol, op.T, crhs)


def solution(mesh):
    sizes = (mesh.shape["dom"] // 8, 8, mesh.shape["face"])
    return jax.shard_map(
        functools.partial(per_device, sizes),
        mesh=mesh,
        in_specs=(
            P(None, ("dom", "face")),
            P(None, ("dom", "face")),
            P(None, None, ("dom", "face")),
            P(None, None, ("dom", "face")),
            P(),
            P(None, ("dom", "face")),
            P(None, ("dom", "face")),
            P(("dom", "face")),
            P(("dom", "face")),
        ),
        out_specs=(P(None, ("dom", "face")), P(None, ("dom", "face")), P(None, ("dom", "face"))),
        check_vma=False,
    )
```

```python
import functools

import jax
import jax.numpy as jnp
import numpy as np
from jax import lax
from jax.experimental import pallas as pl
from jax.experimental.pallas import tpu as pltpu
from jax.sharding import PartitionSpec as P

SWEEPS = 2
MESH = pl.DeviceIdType.MESH
WIDTHS = (256, 384, 128)
STARTS = (0, 256, 640)
COLS = 768
SLOT_COL = 255
RHS_COL = 736
F32 = jnp.float32
BF16 = jnp.bfloat16


def line_basis():
    fine_nodes = np.array([-1.0, -1.0 / np.sqrt(5.0), 1.0 / np.sqrt(5.0), 1.0])
    coarse_nodes = np.array([-1.0, 0.0, 1.0])
    basis = np.ones((4, 3))
    for column in range(3):
        for other in range(3):
            if other != column:
                basis[:, column] *= (fine_nodes - coarse_nodes[other]) / (
                    coarse_nodes[column] - coarse_nodes[other]
                )
    return basis


def restrict_table():
    basis = line_basis()
    prolong = (
        basis[:, None, None, :, None, None]
        * basis[None, :, None, None, :, None]
        * basis[None, None, :, None, None, :]
    ).reshape(64, 27)
    return prolong.T.astype(np.float32)


def split_restrict():
    table = restrict_table()
    high = table.astype(BF16).astype(np.float32)
    both = np.zeros((64, 64), np.float32)
    both[:27] = high
    both[32:59] = table - high
    return both


def nt(lhs, rhs):
    return lax.dot_general(lhs, rhs, (((1,), (1,)), ((), ())), preferred_element_type=F32)


def mm(lhs, rhs):
    return jnp.dot(lhs, rhs, preferred_element_type=F32)


def halves(value):
    high = value.astype(BF16)
    return high, (value - high.astype(F32)).astype(BF16)


def reduce_line(v0, v1, v2, v3):
    basis = line_basis()
    outs = []
    for column in range(3):
        total = None
        for value, weight in zip((v0, v1, v2, v3), basis[:, column]):
            if weight == 0.0:
                continue
            term = value if weight == 1.0 else value * np.float32(weight)
            total = term if total is None else total + term
        outs.append(total)
    return outs


def one_hot(mask):
    return jnp.where(mask, 1.0, 0.0).astype(BF16)


def kernel(
    nz,
    nxc,
    ny,
    start_hbm,
    rhs_hbm,
    diag_hbm,
    prec_hbm,
    lift_hbm,
    nb_hbm,
    ori_hbm,
    own_hbm,
    slot_hbm,
    rmat_hbm,
    sol_ref,
    op_ref,
    crhs_ref,
    val,
    rhs_ref,
    diag_ref,
    prec_ref,
    lift_ref,
    nb_ref,
    ori_ref,
    own_ref,
    slot_ref,
    rmat_ref,
    line,
    coarse,
    trace,
    lift_t,
    index,
    turn,
    halo_out,
    halo_in,
    product,
    pick_x,
    move_zx,
    move_xz,
    send_z0,
    send_z1,
    send_z2,
    recv_z0,
    recv_z1,
    recv_z2,
    send_x0,
    send_x1,
    send_x2,
    recv_x0,
    recv_x1,
    recv_x2,
    in_sem,
    zs_sem,
    zr_sem,
    xs_sem,
    xr_sem,
    hs_sem,
    hr_sem,
    near_sem,
    far_sem,
):
    send_z = (send_z0, send_z1, send_z2)
    recv_z = (recv_z0, recv_z1, recv_z2)
    send_x = (send_x0, send_x1, send_x2)
    recv_x = (recv_x0, recv_x1, recv_x2)
    dom = lax.axis_index("dom")
    y = lax.axis_index("face")
    z = lax.div(dom, nxc)
    xc = lax.rem(dom, nxc)
    above = lax.rem(y + 1, ny)
    below = lax.rem(y + ny - 1, ny)
    rows = nz * nxc * 2

    def at_z(shift):
        return (lax.rem(z + shift + nz, nz) * nxc + xc, y)

    barrier = pltpu.get_barrier_semaphore()
    for other in (above, below):
        pl.semaphore_signal(barrier, inc=1, device_id=(dom, other), device_id_type=MESH)
    for shift in (1, -1, 2, -2):
        pl.semaphore_signal(barrier, inc=1, device_id=at_z(shift), device_id_type=MESH)

    @pl.loop(1, nxc)
    def _(step):
        pl.semaphore_signal(
            barrier,
            inc=1,
            device_id=(z * nxc + lax.rem(xc + step, nxc), y),
            device_id_type=MESH,
        )

    pairs = [
        (start_hbm, val),
        (rmat_hbm, rmat_ref),
        (own_hbm, own_ref),
        (slot_hbm, slot_ref),
        (nb_hbm, nb_ref),
        (ori_hbm, ori_ref),
        (lift_hbm, lift_ref),
        (rhs_hbm, rhs_ref),
        (prec_hbm, prec_ref),
    ]
    fetches = [
        pltpu.make_async_copy(src, dst, in_sem.at[place])
        for place, (src, dst) in enumerate(pairs)
    ]
    slabs = [
        pltpu.make_async_copy(
            diag_hbm.at[pl.ds(16 * i, 16)], diag_ref.at[pl.ds(16 * i, 16)], in_sem.at[9 + i]
        )
        for i in range(4)
    ]
    for fetch in fetches[:4] + slabs + fetches[4:]:
        fetch.start()

    lane = lax.broadcasted_iota(jnp.int32, (1, 128), 1)

    def halo_copy(turn_no, side):
        return pltpu.make_async_remote_copy(
            src_ref=halo_out.at[turn_no, side],
            dst_ref=halo_in.at[turn_no, side],
            send_sem=hs_sem.at[turn_no, side],
            recv_sem=hr_sem.at[turn_no, side],
            device_id=(dom, above if side == 0 else below),
            device_id_type=MESH,
        )

    sends_to = (y < ny - 1, y > 0)
    gets_from = (y > 0, y < ny - 1)

    def halo_start(turn_no):
        for side in range(2):
            @pl.when(sends_to[side])
            def _():
                halo_copy(turn_no, side).start()

    def halo_wait(turn_no):
        for side in range(2):
            @pl.when(gets_from[side])
            def _():
                halo_copy(turn_no, side).wait_recv()

    def halo_sent(turn_no):
        for side in range(2):
            @pl.when(sends_to[side])
            def _():
                halo_copy(turn_no, side).wait_send()

    def send_halo(turn_no):
        low = jnp.concatenate([val[pl.ds(16 * i, 4), :] for i in range(4)], 0)
        high = jnp.concatenate([val[pl.ds(16 * i + 12, 4), :] for i in range(4)], 0)
        halo_out[turn_no, 0] = pltpu.roll(high, 32, 1)
        halo_out[turn_no, 1] = pltpu.roll(low, 96, 1)

    fetches[0].wait()
    send_halo(0)

    pl.semaphore_wait(barrier, 2 + 4 + nxc - 1)
    halo_start(0)
    if nz > 4:
        for side, shift in enumerate((2, -2)):
            pl.semaphore_signal(
                near_sem.at[side], inc=1, device_id=at_z(shift), device_id_type=MESH
            )

    coarse[pl.ds(728, 40), :] = jnp.zeros((40, 128), F32)
    for fetch in fetches[1:4]:
        fetch.wait()
    rmat = rmat_ref[...]
    for i in range(4):
        slabs[i].wait()
        planes = [[], [], []]
        for j in range(4):
            quad = []
            for k in range(4):
                both = mm(rmat, diag_ref[16 * i + 4 * j + k])
                quad.append(both[:32] + both[32:])
            for c, value in enumerate(reduce_line(*quad)):
                planes[c].append(value)
        for c in range(3):
            for b, value in enumerate(reduce_line(*planes[c])):
                line[9 * i + 3 * b + c] = value
    for bc in range(9):
        for a, value in enumerate(reduce_line(*[line[9 * i + bc] for i in range(4)])):
            place = 27 * (9 * a + bc)
            if place > SLOT_COL:
                coarse[pl.ds(place + 1, 27), :] = value[:27]
            elif place + 27 <= SLOT_COL:
                coarse[pl.ds(place, 27), :] = value[:27]
            else:
                head = SLOT_COL - place
                coarse[pl.ds(place, head), :] = value[:head]
                coarse[pl.ds(SLOT_COL + 1, 27 - head), :] = value[head:27]
    coarse[pl.ds(SLOT_COL, 1), :] = slot_ref[...].astype(F32)

    own = own_ref[...]
    own_cols = jnp.broadcast_to(own, (128, 128))
    own_rows = own_cols.T
    row_id = lax.broadcasted_iota(jnp.int32, (128, 128), 0)
    col_id = lax.broadcasted_iota(jnp.int32, (128, 128), 1)
    same = (own_rows == own_cols) & (row_id >= 32) & (row_id < col_id)
    rank = jnp.sum(jnp.where(same, 1.0, 0.0), axis=0, keepdims=True)
    key = jnp.where(lane >= 32, own * 2 + rank.astype(jnp.int32), -1)
    out_rows = lax.broadcasted_iota(jnp.int32, (rows, 128), 0)
    pick_z = one_hot(out_rows == key)

    def columns(chunk):
        return coarse[pl.ds(STARTS[chunk], WIDTHS[chunk]), :].astype(BF16)

    packed = nt(pick_z, columns(0)).astype(BF16)
    send_z[0][...] = packed.reshape(nz, nxc * 2, WIDTHS[0])

    def z_copy(chunk, shift):
        other = lax.rem(z + shift + nz, nz)
        return pltpu.make_async_remote_copy(
            src_ref=send_z[chunk].at[other],
            dst_ref=recv_z[chunk].at[z],
            send_sem=zs_sem.at[chunk],
            recv_sem=zr_sem.at[chunk],
            device_id=(other * nxc + xc, y),
            device_id_type=MESH,
        )

    def z_all(chunk):
        return pltpu.make_async_remote_copy(
            src_ref=send_z[chunk].at[pl.ds(0, nz - 1)],
            dst_ref=recv_z[chunk].at[pl.ds(0, nz - 1)],
            send_sem=zs_sem.at[chunk],
            recv_sem=zr_sem.at[chunk],
            device_id=at_z(1),
            device_id_type=MESH,
        )

    def x_copy(chunk, step):
        other = lax.rem(xc + step, nxc)
        return pltpu.make_async_remote_copy(
            src_ref=send_x[chunk].at[other],
            dst_ref=recv_x[chunk].at[xc],
            send_sem=xs_sem.at[chunk],
            recv_sem=xr_sem.at[chunk],
            device_id=(z * nxc + other, y),
            device_id_type=MESH,
        )

    def x_all(chunk):
        return pltpu.make_async_remote_copy(
            src_ref=send_x[chunk].at[pl.ds(0, nxc - 1)],
            dst_ref=recv_x[chunk].at[pl.ds(0, nxc - 1)],
            send_sem=xs_sem.at[chunk],
            recv_sem=xr_sem.at[chunk],
            device_id=(z * nxc + lax.rem(xc + 1, nxc), y),
            device_id_type=MESH,
        )

    def z_pair(chunk, shift):
        z_copy(chunk, shift).start()
        if 2 * shift != nz:
            z_copy(chunk, -shift).start()

    def start_x(chunk):
        @pl.loop(1, nxc)
        def _(step):
            x_copy(chunk, step).start()

        recv_x[chunk][xc] = send_x[chunk][xc]

    def pack_x(chunk):
        packed = nt(pick_x[...], columns(chunk)).astype(BF16)
        send_x[chunk][...] = packed.reshape(nxc, nz * 2, WIDTHS[chunk])
        start_x(chunk)

    half = nz // 2
    for shift in range(1, min(2, half) + 1):
        z_pair(0, shift)
    s = lax.broadcasted_iota(jnp.int32, (rows, 128), 0)
    deep = 2 * nz
    wide = 2 * nxc
    target = (((s & (deep - 1)) >> 1) * wide) + ((s // deep) * 2) + (s & 1)
    pick_x[...] = one_hot(target == key)
    pack_x(1)
    if nz > 4:
        for side in range(2):
            pl.semaphore_wait(near_sem.at[side], 1)
        if nz > 8:
            for side, shift in enumerate((4, -4)):
                pl.semaphore_signal(
                    far_sem.at[side], inc=1, device_id=at_z(shift), device_id_type=MESH
                )
        for shift in range(3, min(4, half) + 1):
            z_pair(0, shift)
    recv_z[0][z] = send_z[0][z]

    s = lax.broadcasted_iota(jnp.int32, (rows, rows), 0)
    q = lax.broadcasted_iota(jnp.int32, (rows, rows), 1)
    target = (((s & (deep - 1)) >> 1) * wide) + ((s // deep) * 2) + (s & 1)
    move_zx[...] = one_hot(q == target)
    target = (((s & (wide - 1)) >> 1) * deep) + ((s // wide) * 2) + (s & 1)
    move_xz[...] = one_hot(q == target)

    def onward(chunk):
        x_all(chunk).wait_recv()
        table = recv_x[chunk][...].reshape(rows, WIDTHS[chunk])
        moved = mm(move_xz[...], table).astype(BF16)
        send_z[chunk][...] = moved.reshape(nz, nxc * 2, WIDTHS[chunk])
        recv_z[chunk][z] = send_z[chunk][z]

    for fetch in fetches[4:7]:
        fetch.wait()
    trace[...] = jnp.zeros((128, 128), F32)
    lift_t[...] = jnp.zeros((128, 128), F32)
    for f in range(6):
        lift_t[pl.ds(f, 16, stride=8), :] = jnp.concatenate(
            [lift_ref[f], jnp.zeros((16, 64), F32)], 1
        )
    lift_hi, lift_lo = halves(lift_t[...].T[:64])
    index[...] = jnp.zeros((8, 128), jnp.int32)
    turn[...] = jnp.zeros((8, 128), jnp.int32)
    index[pl.ds(0, 6), :] = nb_ref[...] & 127
    turn[pl.ds(0, 6), :] = ori_ref[...]
    idx = index[...]
    flip_row = (turn[...] & 1) != 0
    flip_col = (turn[...] & 2) != 0
    swap = (turn[...] & 4) != 0
    face_id = lax.broadcasted_iota(jnp.int32, (8, 128), 0)
    lane8 = lax.broadcasted_iota(jnp.int32, (8, 128), 1)
    from_low = (face_id == 2) & (lane8 < 32)
    from_high = (face_id == 3) & (lane8 >= 96)

    def matvec(matrix_ref, vector):
        for block in range(8):
            part = matrix_ref[pl.ds(8 * block, 8)].astype(F32) * vector[None]
            product[pl.ds(8 * block, 8), :] = jnp.sum(part, axis=1)
        return product[...]

    def coupled(turn_no):
        trace[pl.ds(1, 16, stride=8), :] = val[pl.ds(0, 16), :]
        trace[pl.ds(0, 16, stride=8), :] = val[pl.ds(48, 16), :]
        for i in range(4):
            trace[pl.ds(32 * i + 3, 4, stride=8), :] = val[pl.ds(16 * i, 4), :]
            trace[pl.ds(32 * i + 2, 4, stride=8), :] = val[pl.ds(16 * i + 12, 4), :]
        trace[pl.ds(5, 16, stride=8), :] = val[pl.ds(0, 16, stride=4), :]
        trace[pl.ds(4, 16, stride=8), :] = val[pl.ds(3, 16, stride=4), :]
        cells = [
            jnp.take_along_axis(
                trace[pl.ds(8 * k, 8), :], idx, axis=1, mode="promise_in_bounds"
            )
            for k in range(16)
        ]
        halo_wait(turn_no)
        low = jnp.where(y > 0, halo_in[turn_no, 0], 0.0)
        high = jnp.where(y < ny - 1, halo_in[turn_no, 1], 0.0)
        cells = [jnp.where(from_low, low[k : k + 1], cells[k]) for k in range(16)]
        cells = [jnp.where(from_high, high[k : k + 1], cells[k]) for k in range(16)]
        cells = [jnp.where(swap, cells[4 * (k % 4) + k // 4], cells[k]) for k in range(16)]
        cells = [jnp.where(flip_row, cells[4 * (3 - k // 4) + k % 4], cells[k]) for k in range(16)]
        cells = [jnp.where(flip_col, cells[4 * (k // 4) + 3 - k % 4], cells[k]) for k in range(16)]
        turned_hi, turned_lo = halves(jnp.concatenate(cells, 0))
        return mm(lift_hi, turned_hi) + (mm(lift_hi, turned_lo) + mm(lift_lo, turned_hi))

    def smooth(places, resid):
        for place in places:
            part = prec_ref[pl.ds(place, 4)].astype(F32) * resid[None]
            val[pl.ds(place, 4), :] = val[pl.ds(place, 4), :] + jnp.sum(part, axis=1)

    edges = [16 * i + j for i in range(4) for j in (0, 12)]
    inner = [16 * i + j for i in range(4) for j in (4, 8)]
    if nz > 8:
        for side in range(2):
            pl.semaphore_wait(far_sem.at[side], 1)
        for shift in range(half, 4, -1):
            z_pair(0, shift)
    fetches[7].wait()
    for sweep in range(SWEEPS):
        through = rhs_ref[...] - matvec(diag_ref, val[...])
        resid = through + coupled(sweep)
        if sweep == 0:
            fetches[8].wait()
        smooth(edges, resid)
        send_halo(sweep + 1)
        halo_start(sweep + 1)
        smooth(inner, resid)
        if sweep == 0:
            onward(1)
            for shift in range(half, 0, -1):
                z_pair(1, shift)
    sol_ref[...] = val[...]
    through = rhs_ref[...] - matvec(diag_ref, val[...])
    resid = through + coupled(SWEEPS)
    both = mm(rmat, resid.astype(BF16))
    coarse[pl.ds(RHS_COL, 32), :] = both[:32] + both[32:]
    pack_x(2)

    agg_rows = lax.broadcasted_iota(jnp.int32, (64, 128), 0)
    stay = one_hot((agg_rows == slot_ref[...]) & (lane < 32))
    stay_hi, stay_lo = halves(coarse[...])
    staying = nt(stay, stay_hi) + nt(stay, stay_lo)

    onward(2)
    for shift in range(half, 0, -1):
        z_pair(2, shift)

    z_all(0).wait_recv()
    table = recv_z[0][...].reshape(rows, WIDTHS[0])
    moved = mm(move_zx[...], table).astype(BF16)
    send_x[0][...] = moved.reshape(nxc, nz * 2, WIDTHS[0])
    start_x(0)

    x_all(0).wait_recv()
    table = recv_x[0][...].reshape(rows, WIDTHS[0])
    want = lax.broadcasted_iota(jnp.int32, (8, WIDTHS[0]), 1) == SLOT_COL
    slots = nt(one_hot(want), table)[:1]
    agg = lax.broadcasted_iota(jnp.int32, (64, rows), 0)
    gather = one_hot(agg == slots.astype(jnp.int32))
    gather_zx = mm(gather, move_zx[...]).astype(BF16)
    total = mm(gather, table) + staying[:, : WIDTHS[0]]
    op_ref[:, pl.ds(0, SLOT_COL)] = total[:, :SLOT_COL]
    z_all(1).wait_recv()
    table = recv_z[1][...].reshape(rows, WIDTHS[1])
    total = mm(gather_zx, table) + staying[:, STARTS[1] : STARTS[2]]
    op_ref[:, pl.ds(SLOT_COL, WIDTHS[1])] = total

    for chunk in range(3):
        z_all(chunk).wait_send()
        x_all(chunk).wait_send()
    for turn_no in range(SWEEPS + 1):
        halo_sent(turn_no)

    z_all(2).wait_recv()
    table = recv_z[2][...].reshape(rows, WIDTHS[2])
    total = mm(gather_zx, table) + staying[:, STARTS[2] :]
    tail = 729 - SLOT_COL - WIDTHS[1]
    op_ref[:, pl.ds(729 - tail, tail)] = total[:, :tail]
    place = RHS_COL - STARTS[2]
    crhs_ref[...] = total.T[place : place + 27]


def hand_over(sol_in, op_in, crhs_in, sol_ref, op_ref, crhs_ref):
    sol_ref[...] = sol_in[...]
    op_ref[...] = op_in[...]
    crhs_ref[...] = crhs_in[...]


def per_device(sizes, start, rhs, diag_block, precond, lift, neighbour, orient, owner, slot):
    nz, nxc, ny = sizes
    rows = nz * nxc * 2
    vmem = pl.BlockSpec(memory_space=pltpu.VMEM)
    anywhere = pl.BlockSpec(memory_space=pltpu.HBM)
    rmat = jnp.asarray(split_restrict().astype(BF16))
    scratch = [
        pltpu.VMEM((64, 128), F32),
        pltpu.VMEM((64, 128), F32),
        pltpu.VMEM((64, 64, 128), BF16),
        pltpu.VMEM((64, 64, 128), BF16),
        pltpu.VMEM((6, 16, 64), F32),
        pltpu.VMEM((6, 128), jnp.int32),
        pltpu.VMEM((6, 128), jnp.int32),
        pltpu.VMEM((1, 128), jnp.int32),
        pltpu.VMEM((1, 128), jnp.int32),
        pltpu.VMEM((64, 64), BF16),
        pltpu.VMEM((36, 32, 128), F32),
        pltpu.VMEM((COLS, 128), F32),
        pltpu.VMEM((128, 128), F32),
        pltpu.VMEM((128, 128), F32),
        pltpu.VMEM((8, 128), jnp.int32),
        pltpu.VMEM((8, 128), jnp.int32),
        pltpu.VMEM((SWEEPS + 1, 2, 16, 128), F32),
        pltpu.VMEM((SWEEPS + 1, 2, 16, 128), F32),
        pltpu.VMEM((64, 128), F32),
        pltpu.VMEM((rows, 128), BF16),
        pltpu.VMEM((rows, rows), BF16),
        pltpu.VMEM((rows, rows), BF16),
    ]
    for blocks, depth in ((nz, nxc * 2), (nz, nxc * 2), (nxc, nz * 2), (nxc, nz * 2)):
        scratch += [pltpu.VMEM((blocks, depth, width), BF16) for width in WIDTHS]
    scratch += [
        pltpu.SemaphoreType.DMA((13,)),
        pltpu.SemaphoreType.DMA((3,)),
        pltpu.SemaphoreType.DMA((3,)),
        pltpu.SemaphoreType.DMA((3,)),
        pltpu.SemaphoreType.DMA((3,)),
        pltpu.SemaphoreType.DMA((SWEEPS + 1, 2)),
        pltpu.SemaphoreType.DMA((SWEEPS + 1, 2)),
        pltpu.SemaphoreType.REGULAR((2,)),
        pltpu.SemaphoreType.REGULAR((2,)),
    ]
    parts = pl.pallas_call(
        functools.partial(kernel, nz, nxc, ny),
        out_shape=(
            jax.ShapeDtypeStruct((64, 128), F32),
            jax.ShapeDtypeStruct((64, 729), F32),
            jax.ShapeDtypeStruct((27, 64), F32),
        ),
        in_specs=[anywhere] * 10,
        out_specs=(vmem, vmem, vmem),
        scratch_shapes=scratch,
        compiler_params=pltpu.CompilerParams(
            collective_id=0, has_side_effects=True, vmem_limit_bytes=60 * 1024 * 1024
        ),
    )(
        start,
        rhs,
        diag_block,
        precond,
        lift,
        neighbour,
        orient,
        owner.reshape(1, -1),
        slot.reshape(1, -1),
        rmat,
    )
    sol, op, crhs = pl.pallas_call(
        hand_over,
        out_shape=tuple(jax.ShapeDtypeStruct(part.shape, F32) for part in parts),
        in_specs=[vmem] * 3,
        out_specs=(vmem, vmem, vmem),
    )(*parts)
    return (sol, op.T, crhs)


def solution(mesh):
    sizes = (mesh.shape["dom"] // 8, 8, mesh.shape["face"])
    return jax.shard_map(
        functools.partial(per_device, sizes),
        mesh=mesh,
        in_specs=(
            P(None, ("dom", "face")),
            P(None, ("dom", "face")),
            P(None, None, ("dom", "face")),
            P(None, None, ("dom", "face")),
            P(),
            P(None, ("dom", "face")),
            P(None, ("dom", "face")),
            P(("dom", "face")),
            P(("dom", "face")),
        ),
        out_specs=(P(None, ("dom", "face")), P(None, ("dom", "face")), P(None, ("dom", "face"))),
        check_vma=False,
    )
```

```python
import functools

import jax
import jax.numpy as jnp
import numpy as np
from jax import lax
from jax.experimental import pallas as pl
from jax.experimental.pallas import tpu as pltpu
from jax.sharding import PartitionSpec as P

SWEEPS = 2
MESH = pl.DeviceIdType.MESH
WIDTHS = (256, 384, 128)
STARTS = (0, 256, 640)
COLS = 768
SLOT_COL = 255
RHS_COL = 736
F32 = jnp.float32
BF16 = jnp.bfloat16


def line_basis():
    fine_nodes = np.array([-1.0, -1.0 / np.sqrt(5.0), 1.0 / np.sqrt(5.0), 1.0])
    coarse_nodes = np.array([-1.0, 0.0, 1.0])
    basis = np.ones((4, 3))
    for column in range(3):
        for other in range(3):
            if other != column:
                basis[:, column] *= (fine_nodes - coarse_nodes[other]) / (
                    coarse_nodes[column] - coarse_nodes[other]
                )
    return basis


def restrict_table():
    basis = line_basis()
    prolong = (
        basis[:, None, None, :, None, None]
        * basis[None, :, None, None, :, None]
        * basis[None, None, :, None, None, :]
    ).reshape(64, 27)
    return prolong.T.astype(np.float32)


def split_restrict():
    table = restrict_table()
    high = table.astype(BF16).astype(np.float32)
    both = np.zeros((64, 64), np.float32)
    both[:27] = high
    both[32:59] = table - high
    return both


def nt(lhs, rhs):
    return lax.dot_general(lhs, rhs, (((1,), (1,)), ((), ())), preferred_element_type=F32)


def mm(lhs, rhs):
    return jnp.dot(lhs, rhs, preferred_element_type=F32)


def halves(value):
    high = value.astype(BF16)
    return high, (value - high.astype(F32)).astype(BF16)


def reduce_line(v0, v1, v2, v3):
    basis = line_basis()
    outs = []
    for column in range(3):
        total = None
        for value, weight in zip((v0, v1, v2, v3), basis[:, column]):
            if weight == 0.0:
                continue
            term = value if weight == 1.0 else value * np.float32(weight)
            total = term if total is None else total + term
        outs.append(total)
    return outs


def one_hot(mask):
    return jnp.where(mask, 1.0, 0.0).astype(BF16)


def kernel(
    nz,
    nxc,
    ny,
    start_hbm,
    rhs_hbm,
    diag_hbm,
    prec_hbm,
    lift_hbm,
    nb_hbm,
    ori_hbm,
    own_hbm,
    slot_hbm,
    rmat_hbm,
    sol_ref,
    op_ref,
    crhs_ref,
    val,
    rhs_ref,
    diag_ref,
    prec_ref,
    lift_ref,
    nb_ref,
    ori_ref,
    own_ref,
    slot_ref,
    rmat_ref,
    line,
    coarse,
    trace,
    lift_t,
    index,
    turn,
    halo_out,
    halo_in,
    product,
    pick_x,
    move_zx,
    move_xz,
    send_z0,
    send_z1,
    send_z2,
    recv_z0,
    recv_z1,
    recv_z2,
    send_x0,
    send_x1,
    send_x2,
    recv_x0,
    recv_x1,
    recv_x2,
    in_sem,
    zs_sem,
    zr_sem,
    xs_sem,
    xr_sem,
    hs_sem,
    hr_sem,
    far_sem,
):
    send_z = (send_z0, send_z1, send_z2)
    recv_z = (recv_z0, recv_z1, recv_z2)
    send_x = (send_x0, send_x1, send_x2)
    recv_x = (recv_x0, recv_x1, recv_x2)
    dom = lax.axis_index("dom")
    y = lax.axis_index("face")
    z = lax.div(dom, nxc)
    xc = lax.rem(dom, nxc)
    above = lax.rem(y + 1, ny)
    below = lax.rem(y + ny - 1, ny)
    rows = nz * nxc * 2

    def at_z(shift):
        return (lax.rem(z + shift + nz, nz) * nxc + xc, y)

    barrier = pltpu.get_barrier_semaphore()
    for other in (above, below):
        pl.semaphore_signal(barrier, inc=1, device_id=(dom, other), device_id_type=MESH)
    for shift in (1, -1, 2, -2, 3, -3, 4, -4):
        pl.semaphore_signal(barrier, inc=1, device_id=at_z(shift), device_id_type=MESH)

    @pl.loop(1, nxc)
    def _(step):
        pl.semaphore_signal(
            barrier,
            inc=1,
            device_id=(z * nxc + lax.rem(xc + step, nxc), y),
            device_id_type=MESH,
        )

    pairs = [
        (start_hbm, val),
        (rmat_hbm, rmat_ref),
        (own_hbm, own_ref),
        (slot_hbm, slot_ref),
        (nb_hbm, nb_ref),
        (ori_hbm, ori_ref),
        (lift_hbm, lift_ref),
        (rhs_hbm, rhs_ref),
        (prec_hbm, prec_ref),
    ]
    fetches = [
        pltpu.make_async_copy(src, dst, in_sem.at[place])
        for place, (src, dst) in enumerate(pairs)
    ]
    slabs = [
        pltpu.make_async_copy(
            diag_hbm.at[pl.ds(16 * i, 16)], diag_ref.at[pl.ds(16 * i, 16)], in_sem.at[9 + i]
        )
        for i in range(4)
    ]
    for fetch in fetches[:4] + slabs + fetches[4:]:
        fetch.start()

    lane = lax.broadcasted_iota(jnp.int32, (1, 128), 1)

    def halo_copy(turn_no, side):
        return pltpu.make_async_remote_copy(
            src_ref=halo_out.at[turn_no, side],
            dst_ref=halo_in.at[turn_no, side],
            send_sem=hs_sem.at[turn_no, side],
            recv_sem=hr_sem.at[turn_no, side],
            device_id=(dom, above if side == 0 else below),
            device_id_type=MESH,
        )

    sends_to = (y < ny - 1, y > 0)
    gets_from = (y > 0, y < ny - 1)

    def halo_start(turn_no):
        for side in range(2):
            @pl.when(sends_to[side])
            def _():
                halo_copy(turn_no, side).start()

    def halo_wait(turn_no):
        for side in range(2):
            @pl.when(gets_from[side])
            def _():
                halo_copy(turn_no, side).wait_recv()

    def halo_sent(turn_no):
        for side in range(2):
            @pl.when(sends_to[side])
            def _():
                halo_copy(turn_no, side).wait_send()

    def send_halo(turn_no):
        low = jnp.concatenate([val[pl.ds(16 * i, 4), :] for i in range(4)], 0)
        high = jnp.concatenate([val[pl.ds(16 * i + 12, 4), :] for i in range(4)], 0)
        halo_out[turn_no, 0] = pltpu.roll(high, 32, 1)
        halo_out[turn_no, 1] = pltpu.roll(low, 96, 1)

    fetches[0].wait()
    send_halo(0)

    pl.semaphore_wait(barrier, 2 + 8 + nxc - 1)
    halo_start(0)
    if nz > 8:
        for side, shift in enumerate((4, -4)):
            pl.semaphore_signal(
                far_sem.at[side], inc=1, device_id=at_z(shift), device_id_type=MESH
            )

    coarse[pl.ds(728, 40), :] = jnp.zeros((40, 128), F32)
    for fetch in fetches[1:4]:
        fetch.wait()
    rmat = rmat_ref[...]
    for i in range(4):
        slabs[i].wait()
        planes = [[], [], []]
        for j in range(4):
            quad = []
            for k in range(4):
                both = mm(rmat, diag_ref[16 * i + 4 * j + k])
                quad.append(both[:32] + both[32:])
            for c, value in enumerate(reduce_line(*quad)):
                planes[c].append(value)
        for c in range(3):
            for b, value in enumerate(reduce_line(*planes[c])):
                line[9 * i + 3 * b + c] = value
    for bc in range(9):
        for a, value in enumerate(reduce_line(*[line[9 * i + bc] for i in range(4)])):
            place = 27 * (9 * a + bc)
            if place > SLOT_COL:
                coarse[pl.ds(place + 1, 27), :] = value[:27]
            elif place + 27 <= SLOT_COL:
                coarse[pl.ds(place, 27), :] = value[:27]
            else:
                head = SLOT_COL - place
                coarse[pl.ds(place, head), :] = value[:head]
                coarse[pl.ds(SLOT_COL + 1, 27 - head), :] = value[head:27]
    coarse[pl.ds(SLOT_COL, 1), :] = slot_ref[...].astype(F32)

    own = own_ref[...]
    own_cols = jnp.broadcast_to(own, (128, 128))
    own_rows = own_cols.T
    row_id = lax.broadcasted_iota(jnp.int32, (128, 128), 0)
    col_id = lax.broadcasted_iota(jnp.int32, (128, 128), 1)
    same = (own_rows == own_cols) & (row_id >= 32) & (row_id < col_id)
    rank = jnp.sum(jnp.where(same, 1.0, 0.0), axis=0, keepdims=True)
    key = jnp.where(lane >= 32, own * 2 + rank.astype(jnp.int32), -1)
    out_rows = lax.broadcasted_iota(jnp.int32, (rows, 128), 0)
    pick_z = one_hot(out_rows == key)

    def columns(chunk):
        return coarse[pl.ds(STARTS[chunk], WIDTHS[chunk]), :].astype(BF16)

    packed = nt(pick_z, columns(0)).astype(BF16)
    send_z[0][...] = packed.reshape(nz, nxc * 2, WIDTHS[0])

    def z_copy(chunk, shift):
        other = lax.rem(z + shift + nz, nz)
        return pltpu.make_async_remote_copy(
            src_ref=send_z[chunk].at[other],
            dst_ref=recv_z[chunk].at[z],
            send_sem=zs_sem.at[chunk],
            recv_sem=zr_sem.at[chunk],
            device_id=(other * nxc + xc, y),
            device_id_type=MESH,
        )

    def z_all(chunk):
        return pltpu.make_async_remote_copy(
            src_ref=send_z[chunk].at[pl.ds(0, nz - 1)],
            dst_ref=recv_z[chunk].at[pl.ds(0, nz - 1)],
            send_sem=zs_sem.at[chunk],
            recv_sem=zr_sem.at[chunk],
            device_id=at_z(1),
            device_id_type=MESH,
        )

    def x_copy(chunk, step):
        other = lax.rem(xc + step, nxc)
        return pltpu.make_async_remote_copy(
            src_ref=send_x[chunk].at[other],
            dst_ref=recv_x[chunk].at[xc],
            send_sem=xs_sem.at[chunk],
            recv_sem=xr_sem.at[chunk],
            device_id=(z * nxc + other, y),
            device_id_type=MESH,
        )

    def x_all(chunk):
        return pltpu.make_async_remote_copy(
            src_ref=send_x[chunk].at[pl.ds(0, nxc - 1)],
            dst_ref=recv_x[chunk].at[pl.ds(0, nxc - 1)],
            send_sem=xs_sem.at[chunk],
            recv_sem=xr_sem.at[chunk],
            device_id=(z * nxc + lax.rem(xc + 1, nxc), y),
            device_id_type=MESH,
        )

    def z_pair(chunk, shift):
        z_copy(chunk, shift).start()
        if 2 * shift != nz:
            z_copy(chunk, -shift).start()

    def start_x(chunk):
        @pl.loop(1, nxc)
        def _(step):
            x_copy(chunk, step).start()

        recv_x[chunk][xc] = send_x[chunk][xc]

    def pack_x(chunk):
        packed = nt(pick_x[...], columns(chunk)).astype(BF16)
        send_x[chunk][...] = packed.reshape(nxc, nz * 2, WIDTHS[chunk])
        start_x(chunk)

    half = nz // 2
    for shift in range(1, min(2, half) + 1):
        z_pair(0, shift)
    s = lax.broadcasted_iota(jnp.int32, (rows, 128), 0)
    deep = 2 * nz
    wide = 2 * nxc
    target = (((s & (deep - 1)) >> 1) * wide) + ((s // deep) * 2) + (s & 1)
    pick_x[...] = one_hot(target == key)
    pack_x(1)
    if nz > 4:
        for shift in range(3, min(4, half) + 1):
            z_pair(0, shift)
    recv_z[0][z] = send_z[0][z]

    s = lax.broadcasted_iota(jnp.int32, (rows, rows), 0)
    q = lax.broadcasted_iota(jnp.int32, (rows, rows), 1)
    target = (((s & (deep - 1)) >> 1) * wide) + ((s // deep) * 2) + (s & 1)
    move_zx[...] = one_hot(q == target)
    target = (((s & (wide - 1)) >> 1) * deep) + ((s // wide) * 2) + (s & 1)
    move_xz[...] = one_hot(q == target)

    def onward(chunk):
        x_all(chunk).wait_recv()
        table = recv_x[chunk][...].reshape(rows, WIDTHS[chunk])
        moved = mm(move_xz[...], table).astype(BF16)
        send_z[chunk][...] = moved.reshape(nz, nxc * 2, WIDTHS[chunk])
        recv_z[chunk][z] = send_z[chunk][z]

    for fetch in fetches[4:7]:
        fetch.wait()
    trace[...] = jnp.zeros((128, 128), F32)
    lift_t[...] = jnp.zeros((128, 128), F32)
    for f in range(6):
        lift_t[pl.ds(f, 16, stride=8), :] = jnp.concatenate(
            [lift_ref[f], jnp.zeros((16, 64), F32)], 1
        )
    lift_hi, lift_lo = halves(lift_t[...].T[:64])
    index[...] = jnp.zeros((8, 128), jnp.int32)
    turn[...] = jnp.zeros((8, 128), jnp.int32)
    index[pl.ds(0, 6), :] = nb_ref[...] & 127
    turn[pl.ds(0, 6), :] = ori_ref[...]
    idx = index[...]
    flip_row = (turn[...] & 1) != 0
    flip_col = (turn[...] & 2) != 0
    swap = (turn[...] & 4) != 0
    face_id = lax.broadcasted_iota(jnp.int32, (8, 128), 0)
    lane8 = lax.broadcasted_iota(jnp.int32, (8, 128), 1)
    from_low = (face_id == 2) & (lane8 < 32)
    from_high = (face_id == 3) & (lane8 >= 96)

    def matvec(matrix_ref, vector):
        for block in range(8):
            part = matrix_ref[pl.ds(8 * block, 8)].astype(F32) * vector[None]
            product[pl.ds(8 * block, 8), :] = jnp.sum(part, axis=1)
        return product[...]

    def coupled(turn_no, meanwhile):
        trace[pl.ds(1, 16, stride=8), :] = val[pl.ds(0, 16), :]
        trace[pl.ds(0, 16, stride=8), :] = val[pl.ds(48, 16), :]
        for i in range(4):
            trace[pl.ds(32 * i + 3, 4, stride=8), :] = val[pl.ds(16 * i, 4), :]
            trace[pl.ds(32 * i + 2, 4, stride=8), :] = val[pl.ds(16 * i + 12, 4), :]
        trace[pl.ds(5, 16, stride=8), :] = val[pl.ds(0, 16, stride=4), :]
        trace[pl.ds(4, 16, stride=8), :] = val[pl.ds(3, 16, stride=4), :]
        cells = [
            jnp.take_along_axis(
                trace[pl.ds(8 * k, 8), :], idx, axis=1, mode="promise_in_bounds"
            )
            for k in range(16)
        ]
        meanwhile()
        halo_wait(turn_no)
        low = jnp.where(y > 0, halo_in[turn_no, 0], 0.0)
        high = jnp.where(y < ny - 1, halo_in[turn_no, 1], 0.0)
        cells = [jnp.where(from_low, low[k : k + 1], cells[k]) for k in range(16)]
        cells = [jnp.where(from_high, high[k : k + 1], cells[k]) for k in range(16)]
        cells = [jnp.where(swap, cells[4 * (k % 4) + k // 4], cells[k]) for k in range(16)]
        cells = [jnp.where(flip_row, cells[4 * (3 - k // 4) + k % 4], cells[k]) for k in range(16)]
        cells = [jnp.where(flip_col, cells[4 * (k // 4) + 3 - k % 4], cells[k]) for k in range(16)]
        turned_hi, turned_lo = halves(jnp.concatenate(cells, 0))
        return mm(lift_hi, turned_hi) + (mm(lift_hi, turned_lo) + mm(lift_lo, turned_hi))

    def smooth(places, resid):
        for place in places:
            part = prec_ref[pl.ds(place, 4)].astype(F32) * resid[None]
            val[pl.ds(place, 4), :] = val[pl.ds(place, 4), :] + jnp.sum(part, axis=1)

    edges = [16 * i + j for i in range(4) for j in (0, 12)]
    inner = [16 * i + j for i in range(4) for j in (4, 8)]
    def far_sends():
        if nz > 8:
            for side in range(2):
                pl.semaphore_wait(far_sem.at[side], 1)
            for shift in range(half, 4, -1):
                z_pair(0, shift)

    def nothing():
        pass

    hooks = (far_sends, nothing, nothing)
    fetches[7].wait()
    for sweep in range(SWEEPS):
        through = rhs_ref[...] - matvec(diag_ref, val[...])
        resid = through + coupled(sweep, hooks[sweep])
        if sweep == 0:
            fetches[8].wait()
        smooth(edges, resid)
        send_halo(sweep + 1)
        halo_start(sweep + 1)
        smooth(inner, resid)
        if sweep == 0:
            onward(1)
            for shift in range(half, 0, -1):
                z_pair(1, shift)
    sol_ref[...] = val[...]
    through = rhs_ref[...] - matvec(diag_ref, val[...])
    resid = through + coupled(SWEEPS, hooks[SWEEPS])
    both = mm(rmat, resid.astype(BF16))
    coarse[pl.ds(RHS_COL, 32), :] = both[:32] + both[32:]
    pack_x(2)

    agg_rows = lax.broadcasted_iota(jnp.int32, (64, 128), 0)
    stay = one_hot((agg_rows == slot_ref[...]) & (lane < 32))
    stay_hi, stay_lo = halves(coarse[...])
    staying = nt(stay, stay_hi) + nt(stay, stay_lo)

    onward(2)
    for shift in range(half, 0, -1):
        z_pair(2, shift)

    z_all(0).wait_recv()
    table = recv_z[0][...].reshape(rows, WIDTHS[0])
    moved = mm(move_zx[...], table).astype(BF16)
    send_x[0][...] = moved.reshape(nxc, nz * 2, WIDTHS[0])
    start_x(0)

    x_all(0).wait_recv()
    table = recv_x[0][...].reshape(rows, WIDTHS[0])
    want = lax.broadcasted_iota(jnp.int32, (8, WIDTHS[0]), 1) == SLOT_COL
    slots = nt(one_hot(want), table)[:1]
    agg = lax.broadcasted_iota(jnp.int32, (64, rows), 0)
    gather = one_hot(agg == slots.astype(jnp.int32))
    gather_zx = mm(gather, move_zx[...]).astype(BF16)
    total = mm(gather, table) + staying[:, : WIDTHS[0]]
    op_ref[:, pl.ds(0, SLOT_COL)] = total[:, :SLOT_COL]
    z_all(1).wait_recv()
    table = recv_z[1][...].reshape(rows, WIDTHS[1])
    total = mm(gather_zx, table) + staying[:, STARTS[1] : STARTS[2]]
    op_ref[:, pl.ds(SLOT_COL, WIDTHS[1])] = total

    for chunk in range(3):
        z_all(chunk).wait_send()
        x_all(chunk).wait_send()
    for turn_no in range(SWEEPS + 1):
        halo_sent(turn_no)

    z_all(2).wait_recv()
    table = recv_z[2][...].reshape(rows, WIDTHS[2])
    total = mm(gather_zx, table) + staying[:, STARTS[2] :]
    tail = 729 - SLOT_COL - WIDTHS[1]
    op_ref[:, pl.ds(729 - tail, tail)] = total[:, :tail]
    place = RHS_COL - STARTS[2]
    crhs_ref[...] = total.T[place : place + 27]


def hand_over(sol_in, op_in, crhs_in, sol_ref, op_ref, crhs_ref):
    sol_ref[...] = sol_in[...]
    op_ref[...] = op_in[...]
    crhs_ref[...] = crhs_in[...]


def per_device(sizes, start, rhs, diag_block, precond, lift, neighbour, orient, owner, slot):
    nz, nxc, ny = sizes
    rows = nz * nxc * 2
    vmem = pl.BlockSpec(memory_space=pltpu.VMEM)
    anywhere = pl.BlockSpec(memory_space=pltpu.HBM)
    rmat = jnp.asarray(split_restrict().astype(BF16))
    scratch = [
        pltpu.VMEM((64, 128), F32),
        pltpu.VMEM((64, 128), F32),
        pltpu.VMEM((64, 64, 128), BF16),
        pltpu.VMEM((64, 64, 128), BF16),
        pltpu.VMEM((6, 16, 64), F32),
        pltpu.VMEM((6, 128), jnp.int32),
        pltpu.VMEM((6, 128), jnp.int32),
        pltpu.VMEM((1, 128), jnp.int32),
        pltpu.VMEM((1, 128), jnp.int32),
        pltpu.VMEM((64, 64), BF16),
        pltpu.VMEM((36, 32, 128), F32),
        pltpu.VMEM((COLS, 128), F32),
        pltpu.VMEM((128, 128), F32),
        pltpu.VMEM((128, 128), F32),
        pltpu.VMEM((8, 128), jnp.int32),
        pltpu.VMEM((8, 128), jnp.int32),
        pltpu.VMEM((SWEEPS + 1, 2, 16, 128), F32),
        pltpu.VMEM((SWEEPS + 1, 2, 16, 128), F32),
        pltpu.VMEM((64, 128), F32),
        pltpu.VMEM((rows, 128), BF16),
        pltpu.VMEM((rows, rows), BF16),
        pltpu.VMEM((rows, rows), BF16),
    ]
    for blocks, depth in ((nz, nxc * 2), (nz, nxc * 2), (nxc, nz * 2), (nxc, nz * 2)):
        scratch += [pltpu.VMEM((blocks, depth, width), BF16) for width in WIDTHS]
    scratch += [
        pltpu.SemaphoreType.DMA((13,)),
        pltpu.SemaphoreType.DMA((3,)),
        pltpu.SemaphoreType.DMA((3,)),
        pltpu.SemaphoreType.DMA((3,)),
        pltpu.SemaphoreType.DMA((3,)),
        pltpu.SemaphoreType.DMA((SWEEPS + 1, 2)),
        pltpu.SemaphoreType.DMA((SWEEPS + 1, 2)),
        pltpu.SemaphoreType.REGULAR((2,)),
    ]
    parts = pl.pallas_call(
        functools.partial(kernel, nz, nxc, ny),
        out_shape=(
            jax.ShapeDtypeStruct((64, 128), F32),
            jax.ShapeDtypeStruct((64, 729), F32),
            jax.ShapeDtypeStruct((27, 64), F32),
        ),
        in_specs=[anywhere] * 10,
        out_specs=(vmem, vmem, vmem),
        scratch_shapes=scratch,
        compiler_params=pltpu.CompilerParams(
            collective_id=0, has_side_effects=True, vmem_limit_bytes=60 * 1024 * 1024
        ),
    )(
        start,
        rhs,
        diag_block,
        precond,
        lift,
        neighbour,
        orient,
        owner.reshape(1, -1),
        slot.reshape(1, -1),
        rmat,
    )
    sol, op, crhs = pl.pallas_call(
        hand_over,
        out_shape=tuple(jax.ShapeDtypeStruct(part.shape, F32) for part in parts),
        in_specs=[vmem] * 3,
        out_specs=(vmem, vmem, vmem),
    )(*parts)
    return (sol, op.T, crhs)


def solution(mesh):
    sizes = (mesh.shape["dom"] // 8, 8, mesh.shape["face"])
    return jax.shard_map(
        functools.partial(per_device, sizes),
        mesh=mesh,
        in_specs=(
            P(None, ("dom", "face")),
            P(None, ("dom", "face")),
            P(None, None, ("dom", "face")),
            P(None, None, ("dom", "face")),
            P(),
            P(None, ("dom", "face")),
            P(None, ("dom", "face")),
            P(("dom", "face")),
            P(("dom", "face")),
        ),
        out_specs=(P(None, ("dom", "face")), P(None, ("dom", "face")), P(None, ("dom", "face"))),
        check_vma=False,
    )
```
